128 devices in a mesh: ep: 4 (over y), tp: 32 (over z, x, core).
Axes of the slice: x: 4, y: 4, z: 4, core: 2. Of those that a mesh axis runs over, the one named last changes fastest.
Arguments:
- tokens: bfloat16 [1024, 7168], P(('ep', 'tp')), may hold values from -6 to 6
- cotangent: bfloat16 [1024, 7168], P(('ep', 'tp')), may hold values from -6 to 6
- routing: int32 [1024, 2], P(('ep', 'tp')), may hold values from 0 to 7, all different within a row; in each aligned block of 8 rows (0 to 7, 8 to 15, ...) at most 3 rows name the same one
- route_gates: bfloat16 [1024, 2], P(('ep', 'tp')), may hold values from 0.5 to 2.5
- gate_weight: bfloat16 [8, 2048, 7168], P(None, 'tp', 'ep'), may hold values from -0.0625 to 0.0625
- up_weight: bfloat16 [8, 2048, 7168], P(None, 'tp', 'ep'), may hold values from -0.0625 to 0.0625
- down_weight: bfloat16 [8, 2048, 7168], P(None, 'tp', 'ep'), may hold values from -0.125 to 0.125
Outputs:
- token_grad: bfloat16 [1024, 7168], P(('ep', 'tp'))
- route_grad: float32 [1024, 2], P(('ep', 'tp'))
- gate_grad: bfloat16 [8, 2048, 7168], P(None, 'tp', 'ep')
- up_grad: bfloat16 [8, 2048, 7168], P(None, 'tp', 'ep')
- down_grad: bfloat16 [8, 2048, 7168], P(None, 'tp', 'ep')
The draws below stay inside these ranges and needn't reach their ends.
Inputs may be any that keep to these rules, and one draw needn't show every extreme that they name: `routing`: in the rows of one device a row names 2 different experts, no expert is named more than 3 times, a bound that some block reaches.
All inputs are finite; a program needn't handle non-finite values.
Results may differ from the reference program's by a relative error of at most 0.017.
Values may be sent and summed in bfloat16 or wider, within the bound.
No kernel may reach another device: no remote copies, remote signals or barrier semaphores. Data moves between devices by JAX's collectives and lax.ppermute only.
A program may use at most 192 MiB of HBM per device.

```python
import math
import jax
import jax.numpy as jnp
import numpy as np
from jax import lax

D = 7168
H = 2048
E = 8
TOP = 2
TOK_DEV = 8
MOST = 3
HS = 64
TOKENS = 1024
N_EP = 4
N_TP = 32


def level_of(stream_key, dims, split, low, top_value):
    gain = 1.0
    for dim, shards_of in split:
        draws = jax.random.uniform(jax.random.fold_in(jax.random.fold_in(stream_key, 6), dim), (shards_of,), jnp.float32, low / len(split), top_value / len(split))
        gain = gain * jnp.repeat(jnp.exp(draws), dims[dim] // shards_of).reshape((-1,) + (1,) * (len(dims) - 1 - dim))
    return gain


def assign_block(key, own, number, rows, number_of, top, limit, lean):
    sequence = jax.random.permutation(key, number_of)
    crowded, common = shares(number_of, rows * top, limit, lean, True), shares(number_of, rows * top, limit, lean, False)
    places = jnp.arange(number_of)

    def named(sizes, offset_by):
        used = int((sizes > 0).sum())
        fixed = max(1, used // 4)
        shifted = fixed + (places - fixed + offset_by * (used - fixed)) % max(1, number_of - fixed)
        return jnp.zeros((number_of,), jnp.int32).at[sequence[jnp.where(places < fixed, places, shifted)]].set(jnp.asarray(sizes, jnp.int32))

    sizes = jnp.where(number % 4 == 0, named(crowded, number // 4), named(common, number - number // 4 - 1))
    mixed = jax.random.permutation(jax.random.fold_in(own, 3), number_of)
    source_of, sink = mixed[0:number_of // 2 * 2:2], mixed[1:number_of // 2 * 2:2]
    slack = jnp.minimum(sizes[source_of] - 1, limit - sizes[sink]) // 2
    slack = jnp.where((source_of == sequence[0]) | (sink == sequence[0]) | (sizes[sink] == 0), 0, jnp.maximum(slack, 0))
    shifted = jax.random.randint(jax.random.fold_in(own, 4), (number_of // 2,), 0, 1 << 20) % (slack + 1)
    sizes = sizes.at[source_of].add(-shifted).at[sink].add(shifted)
    items = jnp.searchsorted(jnp.cumsum(sizes), jnp.arange(rows * top), side="right").astype(jnp.int32)
    grid = items.reshape(top, rows).T
    grid = grid[jax.random.permutation(jax.random.fold_in(own, 1), rows)]
    offset_by = jax.random.randint(jax.random.fold_in(own, 2), (rows, 1), 0, top)
    return jnp.take_along_axis(grid, (jnp.arange(top)[None, :] + offset_by) % top, axis=1)


def shares(count, total, most, slope, full):
    portions = [(1 << 20) // math.isqrt(rank ** slope) + 1 for rank in range(1, count + 1)]
    largest = most if full else min(most, max(-(-total // count), total * portions[0] // sum(portions)))
    least = 1 if total - largest >= count - 1 else 0
    given, surplus = [largest] + [least] * (count - 1), total - largest - least * (count - 1)
    while surplus > 0:
        free = [i for i in range(1, count) if given[i] < largest] or [i for i in range(1, count) if given[i] < most]
        pool, remaining = sum([portions[i] for i in free]), surplus
        for i in free:
            more = min(most - given[i], max(1, remaining * portions[i] // pool), surplus)
            given[i] = given[i] + more
            surplus = surplus - more
    return np.array(given)


def bell_draw(rng, extent, deviation, most, split=(), kind=jnp.bfloat16):
    result = jax.random.normal(rng, extent, jnp.float32) * deviation
    if len(split) > 0:
        result = level_of(rng, extent, split, -0.22, 0.18) * result
    return jnp.clip(result, min=-most, max=most).astype(kind)


def setup_inputs(seed: int = 0) -> dict:
    keys = jax.random.split(jax.random.key(seed), 8)
    tokens = bell_draw(keys[0], (TOKENS, D), 1.0, 6.0, ((0, 128),))
    cotangent = bell_draw(keys[1], (TOKENS, D), 1.0, 6.0, ((0, 128),))
    routing_keys = jax.random.split(jax.random.fold_in(keys[2], 1), TOKENS // TOK_DEV)
    routing_turns = jax.random.permutation(jax.random.fold_in(keys[2], 3), TOKENS // TOK_DEV)
    routing = jax.vmap(lambda own, number: assign_block(jax.random.fold_in(keys[2], 2), own, number, TOK_DEV, E, TOP, MOST, 2))(routing_keys, routing_turns).reshape((TOKENS, TOP))
    route_gates = jnp.clip(0.5 + 2.0 * jax.random.uniform(keys[3], (TOKENS, TOP), jnp.float32) ** level_of(keys[3], (TOKENS, TOP), ((0, 128),), -0.2, 0.2), 0.5, 2.5).astype(jnp.bfloat16)
    gate_weight = bell_draw(keys[4], (E, H, D), D ** -0.5, 0.0625, ((1, 32), (2, 4)))
    up_weight = bell_draw(keys[5], (E, H, D), D ** -0.5, 0.0625, ((1, 32), (2, 4)))
    down_weight = bell_draw(keys[6], (E, H, D), H ** -0.5, 0.125, ((1, 32), (2, 4)))
    return dict(tokens=tokens, cotangent=cotangent, routing=routing, route_gates=route_gates, gate_weight=gate_weight, up_weight=up_weight, down_weight=down_weight)


def slot_tables(routing):
    devices_all = N_EP * N_TP
    entries = TOK_DEV * TOP
    routes_flat = routing.reshape(devices_all, entries)
    expert_iota = jnp.arange(E, dtype=jnp.int32)
    onehot = (routes_flat[:, :, None] == expert_iota[None, None, :]).astype(jnp.int32)
    before = jnp.cumsum(onehot, axis=1) - onehot
    slot_rank = jnp.sum(before * onehot, axis=2)
    device_ids = jnp.arange(devices_all, dtype=jnp.int32)[:, None]
    slot_index = (device_ids * MOST + slot_rank).reshape(-1).astype(jnp.int32)
    expert_ids = routing.reshape(-1).astype(jnp.int32)
    token_ids = (jnp.arange(TOKENS * TOP, dtype=jnp.int32) // TOP).astype(jnp.int32)
    capacity = devices_all * MOST
    table = jnp.full((E, capacity), TOKENS, jnp.int32).at[expert_ids, slot_index].set(token_ids)
    return expert_ids, slot_index, table


def expert_grads(tokens_pad, cotangent_pad, operands):
    table_row, gate_row, gate_mat, up_mat, down_mat = operands
    rows_x = tokens_pad[table_row]
    rows_dy = cotangent_pad[table_row]
    gate = jnp.dot(rows_x, gate_mat.T, preferred_element_type=jnp.float32)
    upper = jnp.dot(rows_x, up_mat.T, preferred_element_type=jnp.float32)
    hidden = (jax.nn.silu(gate) * upper).astype(jnp.bfloat16)
    factor = gate_row[:, None]
    back = factor * jnp.dot(rows_dy, down_mat.T, preferred_element_type=jnp.float32)
    output = jnp.dot(hidden, down_mat, preferred_element_type=jnp.float32)
    route_term = jnp.sum(rows_dy.astype(jnp.float32) * output, axis=1)
    sigma = jax.nn.sigmoid(gate)
    d_gate = (back * upper * sigma * (1.0 + gate * (1.0 - sigma))).astype(jnp.bfloat16)
    d_up = (back * jax.nn.silu(gate)).astype(jnp.bfloat16)

    def shard_term(total, index):
        start = (index * HS).astype(jnp.int32)
        part_gate = lax.dynamic_slice_in_dim(d_gate, start, HS, 1)
        part_up = lax.dynamic_slice_in_dim(d_up, start, HS, 1)
        mat_gate = lax.dynamic_slice_in_dim(gate_mat, start, HS, 0)
        mat_up = lax.dynamic_slice_in_dim(up_mat, start, HS, 0)
        term = jnp.dot(part_gate, mat_gate, preferred_element_type=jnp.float32)
        term = term + jnp.dot(part_up, mat_up, preferred_element_type=jnp.float32)
        rounded = lax.optimization_barrier(term.astype(jnp.bfloat16))
        return total + rounded.astype(jnp.float32), None

    start_total = jnp.zeros((rows_x.shape[0], D), jnp.float32)
    slot_grad, unused = lax.scan(shard_term, start_total, jnp.arange(H // HS, dtype=jnp.int32))
    grad_gate = jnp.dot(d_gate.T, rows_x, preferred_element_type=jnp.float32).astype(jnp.bfloat16)
    grad_up = jnp.dot(d_up.T, rows_x, preferred_element_type=jnp.float32).astype(jnp.bfloat16)
    scaled = (factor * hidden.astype(jnp.float32)).astype(jnp.bfloat16)
    grad_down = jnp.dot(scaled.T, rows_dy, preferred_element_type=jnp.float32).astype(jnp.bfloat16)
    return slot_grad, route_term, grad_gate, grad_up, grad_down


def partial_expert(tokens_pad, cotangent_pad):
    def apply_one(operands):
        return expert_grads(tokens_pad, cotangent_pad, operands)
    return apply_one


def reference(tokens, cotangent, routing, route_gates, gate_weight, up_weight, down_weight):
    expert_ids, slot_index, table = slot_tables(routing)
    capacity = N_EP * N_TP * MOST
    gate_table = jnp.zeros((E, capacity), jnp.float32).at[expert_ids, slot_index].set(route_gates.reshape(-1).astype(jnp.float32))
    tokens_pad = jnp.concatenate([tokens, jnp.zeros((1, D), tokens.dtype)], axis=0)
    cotangent_pad = jnp.concatenate([cotangent, jnp.zeros((1, D), cotangent.dtype)], axis=0)
    results = lax.map(partial_expert(tokens_pad, cotangent_pad), (table, gate_table, gate_weight, up_weight, down_weight))
    slot_grads, route_terms, gate_grad, up_grad, down_grad = results
    picked = slot_grads[expert_ids, slot_index]
    token_grad = jnp.sum(picked.reshape(TOKENS, TOP, D), axis=1).astype(jnp.bfloat16)
    route_grad = route_terms[expert_ids, slot_index].reshape(TOKENS, TOP)
    return token_grad, route_grad, gate_grad, up_grad, down_grad
```

```python
import jax
import jax.numpy as jnp
from jax import lax
from jax.experimental import pallas as pl
from jax.experimental.pallas import tpu as pltpu
from jax.sharding import Mesh
from jax.sharding import PartitionSpec as P

BF = jnp.bfloat16
F32 = jnp.float32
EXPERTS = 8
HID = 64
COLS = EXPERTS * HID
LANES = 128
PLANE = ("z", "x", "core")
TORUS = ("z", "x", "ep")


def params():
    return pltpu.CompilerParams(vmem_limit_bytes=56 << 20)


def lane_expert(rows):
    lane = lax.broadcasted_iota(jnp.int32, (rows, COLS), 1)
    return (lane // HID).astype(F32)


def first_half(rows):
    return lax.broadcasted_iota(jnp.int32, (rows, LANES), 1) < HID


def pick(full, route_a, route_b, owner, low):
    kept_a = jnp.where(owner == route_a, full, 0.0)
    kept_b = jnp.where(owner == route_b, full, 0.0)
    sum_a = sum(kept_a[:, g * LANES:(g + 1) * LANES] for g in range(COLS // LANES))
    sum_b = sum(kept_b[:, g * LANES:(g + 1) * LANES] for g in range(COLS // LANES))
    sum_a = sum_a + pltpu.roll(sum_a, HID, 1)
    sum_b = sum_b + pltpu.roll(sum_b, HID, 1)
    return jnp.where(low, sum_a, sum_b)


def spread(short, route_a, route_b, owner, low):
    turned = pltpu.roll(short, HID, 1)
    val_a = jnp.where(low, short, turned)
    val_b = jnp.where(low, turned, short)
    groups = COLS // LANES
    wide_a = jnp.concatenate([val_a] * groups, axis=1)
    wide_b = jnp.concatenate([val_b] * groups, axis=1)
    return jnp.where(owner == route_a, wide_a, jnp.where(owner == route_b, wide_b, 0.0))


def dot_t(rows, mat):
    return lax.dot_general(rows, mat, (((1,), (1,)), ((), ())), preferred_element_type=F32)


def pre_two(x_ref, meta_ref, gate_ref, up_ref, out_ref):
    rows = x_ref.shape[0]
    meta = meta_ref[...].astype(F32)
    route_a, route_b = meta[:, 0:1], meta[:, 1:2]
    owner, low = lane_expert(rows), first_half(rows)
    x = x_ref[...]
    out_ref[:, :LANES] = pick(dot_t(x, gate_ref[...]), route_a, route_b, owner, low).astype(BF)
    out_ref[:, LANES:] = pick(dot_t(x, up_ref[...]), route_a, route_b, owner, low).astype(BF)


def pre_one(x_ref, meta_ref, down_ref, out_ref):
    rows = x_ref.shape[0]
    meta = meta_ref[...].astype(F32)
    owner, low = lane_expert(rows), first_half(rows)
    full = dot_t(x_ref[...], down_ref[...])
    out_ref[...] = pick(full, meta[:, 0:1], meta[:, 1:2], owner, low).astype(BF)


def pre_call(body, rows_all, mats, width, outs):
    count = rows_all.shape[0]
    step = 256
    return pl.pallas_call(
        body,
        grid=(count // step,),
        in_specs=[
            pl.BlockSpec((step, width), lambda i: (i, 0)),
            pl.BlockSpec((step, LANES), lambda i: (i, 0)),
        ]
        + [pl.BlockSpec((COLS, width), lambda i: (0, 0))] * len(mats),
        out_specs=pl.BlockSpec((step, outs), lambda i: (i, 0)),
        out_shape=jax.ShapeDtypeStruct((count, outs), BF),
        compiler_params=params(),
    )


def middle(meta_ref, *refs):
    two_refs, one_refs, outs = refs[:4], refs[4:8], refs[8:]
    dgate_ref, dup_ref, scaled_ref, route_ref = outs
    rows = meta_ref.shape[0]
    meta = meta_ref[...].astype(F32)
    route_a, route_b = meta[:, 0:1], meta[:, 1:2]
    owner, low = lane_expert(rows), first_half(rows)
    factor = jnp.where(low, meta[:, 2:3], meta[:, 3:4])
    gate = sum(r[:, :LANES].astype(F32) for r in two_refs)
    upper = sum(r[:, LANES:].astype(F32) for r in two_refs)
    reverse = sum(r[...].astype(F32) for r in one_refs)
    sigma = jax.nn.sigmoid(gate)
    act = gate * sigma
    hidden = (act * upper).astype(BF).astype(F32)
    back = factor * reverse
    d_gate = back * upper * sigma * (1.0 + gate * (1.0 - sigma))
    d_up = back * act
    dgate_ref[...] = spread(d_gate, route_a, route_b, owner, low).astype(BF)
    dup_ref[...] = spread(d_up, route_a, route_b, owner, low).astype(BF)
    scaled_ref[...] = spread(factor * hidden, route_a, route_b, owner, low).astype(BF)
    prod = hidden * reverse
    term_a = jnp.sum(jnp.where(low, prod, 0.0), axis=1, keepdims=True)
    term_b = jnp.sum(jnp.where(low, 0.0, prod), axis=1, keepdims=True)
    lane = lax.broadcasted_iota(jnp.int32, (rows, LANES), 1)
    route_ref[...] = jnp.where(lane == 0, term_a, jnp.where(lane == 1, term_b, 0.0)).astype(BF)


def middle_call(meta_src, width, twos, ones):
    count = meta_src.shape[0]
    step = 256
    row = lambda w: pl.BlockSpec((step, w), lambda i: (i, 0))
    return pl.pallas_call(
        middle,
        grid=(count // step,),
        in_specs=[pl.BlockSpec((step, LANES), lambda i: (i, width // LANES))]
        + [row(2 * LANES)] * 4
        + [row(LANES)] * 4,
        out_specs=[row(COLS), row(COLS), row(COLS), row(LANES)],
        out_shape=[jax.ShapeDtypeStruct((count, COLS), BF)] * 3
        + [jax.ShapeDtypeStruct((count, LANES), BF)],
        compiler_params=params(),
    )(meta_src, *twos, *ones)


def terms(side_ref, dgate_ref, dup_ref, route_ref, gate_ref, up_ref, out_ref):
    blocks, _, rows, width = dgate_ref.shape
    d_gate = dgate_ref[...].reshape(blocks * rows, width)
    d_up = dup_ref[...].reshape(blocks * rows, width)
    total = jnp.dot(d_gate, gate_ref[...], preferred_element_type=F32)
    total = total + jnp.dot(d_up, up_ref[...], preferred_element_type=F32)
    deep = gate_ref.shape[1]
    out_ref[:, :deep] = total.astype(BF)
    out_ref[:, deep:] = route_ref[...].reshape(blocks * rows, LANES)


def terms_call(side, dgate, dup, route, gate, up):
    chips, _, rows, _ = dgate.shape
    take = 8
    width = gate.shape[1]
    view = lambda w: pl.BlockSpec((take, 1, rows, w), lambda i, s: (i, s[0], 0, 0))
    whole = pl.BlockSpec((COLS, width), lambda i, s: (0, 0))
    return pl.pallas_call(
        terms,
        grid_spec=pltpu.PrefetchScalarGridSpec(
            num_scalar_prefetch=1,
            grid=(chips // take,),
            in_specs=[view(COLS), view(COLS), view(LANES), whole, whole],
            out_specs=pl.BlockSpec((take * rows, width + LANES), lambda i, s: (i, 0)),
        ),
        out_shape=jax.ShapeDtypeStruct((chips * rows, width + LANES), BF),
        compiler_params=params(),
    )(side, dgate, dup, route, gate, up)


def around(arr):
    size = lax.axis_size("ep")
    return [arr] + [
        lax.ppermute(arr, "ep", [(i, (i + s) % size) for i in range(size)]) for s in range(1, size)
    ]


def contract_rows(left, right):
    return lax.dot_general(left, right, (((0,), (0,)), ((), ())), preferred_element_type=F32)


def local(tokens, cotangent, routing, route_gates, gate_weight, up_weight, down_weight):
    tok_rows, full = tokens.shape
    width = gate_weight.shape[2]
    planes = full // width
    gate = gate_weight.reshape(COLS, width)
    up = up_weight.reshape(COLS, width)
    down = down_weight.reshape(COLS, width)
    meta = jnp.concatenate([routing.astype(BF), route_gates], axis=1)
    meta = jnp.pad(meta, ((0, 0), (0, LANES - meta.shape[1])))
    slices_x = jnp.swapaxes(tokens.reshape(tok_rows, planes, width), 0, 1)
    meta_all = jnp.broadcast_to(meta[None], (planes, tok_rows, LANES))
    send_x = jnp.concatenate([slices_x, meta_all], axis=2)
    send_y = jnp.swapaxes(cotangent.reshape(tok_rows, planes, width), 0, 1)
    own_x = lax.all_to_all(send_x, "ep", 0, 0, tiled=True).reshape(planes * tok_rows, -1)
    own_y = lax.all_to_all(send_y, "ep", 0, 0, tiled=True).reshape(planes * tok_rows, width)
    all_x = lax.all_gather(own_x, PLANE, axis=0, tiled=True)
    all_y = lax.all_gather(own_y, PLANE, axis=0, tiled=True)
    meta_all = all_x[:, width:]
    two = pre_call(pre_two, all_x, (gate, up), width, 2 * LANES)(all_x, meta_all, gate, up)
    twos = around(two)
    one = pre_call(pre_one, all_y, (down,), width, LANES)(all_y, meta_all, down)
    ones = around(one)
    d_gate, d_up, scaled, route = middle_call(all_x, width, twos, ones)
    cores = lax.axis_size("core")
    split = lambda a: a.reshape(-1, cores, planes * tok_rows, a.shape[1])
    core = lax.axis_index("core").astype(jnp.int32).reshape(1)
    pieces = (split(d_gate), split(d_up), split(route), gate, up)
    theirs = terms_call(1 - core, *pieces)
    got = lax.ppermute(theirs, "core", [(0, 1), (1, 0)])
    mine = terms_call(core, *pieces)
    pair = (mine.astype(F32) + got.astype(F32)).astype(BF)
    parts = lax.all_to_all(
        pair.reshape(-1, tok_rows, width + LANES), TORUS, 0, 0, tiled=True
    )
    total = jnp.sum(parts.reshape(-1, planes, tok_rows, width + LANES).astype(F32), axis=0)
    token_grad = jnp.swapaxes(total[:, :, :width], 0, 1).reshape(tok_rows, full).astype(BF)
    route_grad = total[0, :, width:width + routing.shape[1]]
    x_rows = all_x[:, :width]
    shape = gate_weight.shape
    gate_grad = contract_rows(d_gate, x_rows).astype(BF).reshape(shape)
    up_grad = contract_rows(d_up, x_rows).astype(BF).reshape(shape)
    down_grad = contract_rows(scaled, all_y).astype(BF).reshape(shape)
    return (token_grad, route_grad, gate_grad, up_grad, down_grad)


def solution(mesh):
    names = ("ep", "z", "x", "core")
    fine = Mesh(mesh.devices.reshape(4, 4, 4, 2), names)
    rows = P(names, None)
    mats = P(None, ("z", "x", "core"), "ep")
    return jax.shard_map(
        local,
        mesh=fine,
        in_specs=(rows, rows, rows, rows, mats, mats, mats),
        out_specs=(rows, rows, mats, mats, mats),
        check_vma=False,
    )
```

```python
import jax
import jax.numpy as jnp
from jax import lax
from jax.experimental import pallas as pl
from jax.experimental.pallas import tpu as pltpu
from jax.sharding import Mesh
from jax.sharding import PartitionSpec as P

BF = jnp.bfloat16
F32 = jnp.float32
EXPERTS = 8
HID = 64
COLS = EXPERTS * HID
LANES = 128
SIDE = 4
PLANE = ("z", "x", "core")
TORUS = ("ep", "z", "x")


def params():
    return pltpu.CompilerParams(vmem_limit_bytes=58 << 20)


def first_half(rows):
    return lax.broadcasted_iota(jnp.int32, (rows, LANES), 1) < HID


def dot_t(rows, mat):
    return lax.dot_general(rows, mat, (((1,), (1,)), ((), ())), preferred_element_type=F32)


def flat(ref):
    lead, rows, width = ref.shape
    return ref[...].reshape(lead * rows, width)


def pre_acts(count, width):
    def body(*refs):
        xs, ys, mats = refs[:count], refs[count:2 * count], refs[2 * count:2 * count + 6]
        out_ref, acc_ref = refs[2 * count + 6], refs[2 * count + 7]
        step, steps = pl.program_id(0), pl.num_programs(0)
        rows = xs[0].shape[0] * xs[0].shape[1]
        chunk = mats[0].shape[0]
        lane = lax.broadcasted_iota(jnp.int32, (rows, chunk), 1)
        owner = (lane // HID + step * (chunk // HID)).astype(F32)
        for n in range(count):
            x_all = flat(xs[n])
            x, y = x_all[:, :width], flat(ys[n])
            meta = x_all[:, width:].astype(F32)
            hit_a = owner == meta[:, 0:1]
            hit_b = owner == meta[:, 1:2]
            for m in range(6):
                full = dot_t(y if m % 3 == 2 else x, mats[m][...])
                for k, hit in enumerate((hit_a, hit_b)):
                    kept = jnp.where(hit, full, 0.0)
                    short = sum(kept[:, g * LANES:(g + 1) * LANES] for g in range(chunk // LANES))
                    spot = (n, slice(None), slice((2 * m + k) * LANES, (2 * m + k + 1) * LANES))

                    @pl.when(step == 0)
                    def _():
                        acc_ref[spot] = short

                    @pl.when(step > 0)
                    def _():
                        acc_ref[spot] = acc_ref[spot] + short

        @pl.when(step == steps - 1)
        def _():
            low = first_half(rows)
            for n in range(count):
                for m in range(6):
                    sum_a = acc_ref[n, :, 2 * m * LANES:(2 * m + 1) * LANES]
                    sum_b = acc_ref[n, :, (2 * m + 1) * LANES:(2 * m + 2) * LANES]
                    sum_a = sum_a + pltpu.roll(sum_a, HID, 1)
                    sum_b = sum_b + pltpu.roll(sum_b, HID, 1)
                    val = jnp.where(low, sum_a, sum_b).astype(BF)
                    lead, short_rows = xs[n].shape[0], xs[n].shape[1]
                    val = val.reshape(lead, short_rows, LANES)
                    out_ref[:, n * short_rows:(n + 1) * short_rows, m * LANES:(m + 1) * LANES] = val

    return body


def pre_call(xs, ys, mats):
    count = len(xs)
    lead, rows, _ = xs[0].shape
    width = ys[0].shape[2]
    steps = 2
    whole = lambda a: pl.BlockSpec(a.shape, lambda i: (0,) * a.ndim)
    out = (lead, rows * count, 6 * LANES)
    return pl.pallas_call(
        pre_acts(count, width),
        grid=(steps,),
        in_specs=[whole(a) for a in xs + ys]
        + [pl.BlockSpec((COLS // steps, width), lambda i: (i, 0))] * 6,
        out_specs=pl.BlockSpec(out, lambda i: (0, 0, 0)),
        out_shape=jax.ShapeDtypeStruct(out, BF),
        scratch_shapes=[pltpu.VMEM((count, lead * rows, 12 * LANES), F32)],
        compiler_params=params(),
    )(*xs, *ys, *mats)


def middle(plane_ref, parts_ref, meta_ref, out_ref, route_ref):
    rows = parts_ref.shape[1]
    meta = meta_ref[...].reshape(rows, LANES).astype(F32)
    low = first_half(rows)
    factor = jnp.where(low, meta[:, 2:3], meta[:, 3:4])
    prod = jnp.zeros((rows, LANES), F32)
    for side in range(2):
        vals = []
        for m in range(3):
            at = (3 * side + m) * LANES
            vals.append(sum(parts_ref[j, :, at:at + LANES].astype(F32) for j in range(SIDE)))
        gate, upper, reverse = vals
        sigma = jax.nn.sigmoid(gate)
        act = gate * sigma
        hidden = (act * upper).astype(BF).astype(F32)
        back = factor * reverse
        d_gate = back * upper * sigma * (1.0 + gate * (1.0 - sigma))
        at = 3 * side * LANES
        out_ref[:, at:at + LANES] = d_gate.astype(BF)
        out_ref[:, at + LANES:at + 2 * LANES] = (back * act).astype(BF)
        out_ref[:, at + 2 * LANES:at + 3 * LANES] = (factor * hidden).astype(BF)
        prod = prod + hidden * reverse
    term_a = jnp.sum(jnp.where(low, prod, 0.0), axis=1, keepdims=True)
    term_b = jnp.sum(jnp.where(low, 0.0, prod), axis=1, keepdims=True)
    lane = lax.broadcasted_iota(jnp.int32, (rows, LANES), 1)
    route_ref[...] = jnp.where(lane == 0, term_a, jnp.where(lane == 1, term_b, 0.0)).astype(BF)


def middle_call(plane, parts, meta):
    _, rows, width = parts.shape
    return pl.pallas_call(
        middle,
        grid_spec=pltpu.PrefetchScalarGridSpec(
            num_scalar_prefetch=1,
            grid=(1,),
            in_specs=[
                pl.BlockSpec(parts.shape, lambda i, s: (0, 0, 0)),
                pl.BlockSpec((1, rows, LANES), lambda i, s: (s[0], 0, 0)),
            ],
            out_specs=[
                pl.BlockSpec((rows, width), lambda i, s: (0, 0)),
                pl.BlockSpec((rows, LANES), lambda i, s: (0, 0)),
            ],
        ),
        out_shape=[
            jax.ShapeDtypeStruct((rows, width), BF),
            jax.ShapeDtypeStruct((rows, LANES), BF),
        ],
        compiler_params=params(),
    )(plane, parts, meta)


def spread(short, route_a, route_b, owner, low):
    turned = pltpu.roll(short, HID, 1)
    val_a = jnp.where(low, short, turned)
    val_b = jnp.where(low, turned, short)
    groups = COLS // LANES
    wide_a = jnp.concatenate([val_a] * groups, axis=1)
    wide_b = jnp.concatenate([val_b] * groups, axis=1)
    return jnp.where(owner == route_a, wide_a, jnp.where(owner == route_b, wide_b, 0.0))


def terms(spots_ref, acts_ref, meta_ref, route_ref, *refs):
    mats, out_ref, wides = refs[:4], refs[4], refs[5:]
    lead, rows, _ = acts_ref.shape
    meta = flat(meta_ref).astype(F32)
    acts = flat(acts_ref).astype(F32)
    route_a, route_b = meta[:, 0:1], meta[:, 1:2]
    total_rows = lead * rows
    lane = lax.broadcasted_iota(jnp.int32, (total_rows, COLS), 1)
    owner, low = (lane // HID).astype(F32), first_half(total_rows)
    total = None
    for m in range(6):
        short = acts[:, m * LANES:(m + 1) * LANES]
        wide = spread(short, route_a, route_b, owner, low).astype(BF)
        wides[m][...] = wide
        if m % 3 < 2:
            part = jnp.dot(wide, mats[2 * (m // 3) + m % 3][...], preferred_element_type=F32)
            total = part if total is None else total + part
    deep = mats[0].shape[1]
    plane = spots_ref[16]
    base = pl.program_id(0) * lead
    route = route_ref[...].astype(F32)
    for j in range(lead):
        mine = jnp.where(base + j == plane, 1.0, 0.0)
        for b in range(16):
            at = j * rows + b * 8
            spot = pl.multiple_of(spots_ref[b] * 8, 8)
            out_ref[j, pl.ds(spot, 8), :deep] = total[at:at + 8].astype(BF)
            out_ref[j, pl.ds(spot, 8), deep:] = (route[b * 8:b * 8 + 8] * mine).astype(BF)


def terms_call(spots, acts, meta, route, mats):
    lead, rows, width = acts.shape
    deep = mats[0].shape[1]
    take = 2
    view = lambda w: pl.BlockSpec((take, rows, w), lambda i, s: (i, 0, 0))
    whole = pl.BlockSpec((COLS, deep), lambda i, s: (0, 0))
    wide = pl.BlockSpec((take * rows, COLS), lambda i, s: (i, 0))
    return pl.pallas_call(
        terms,
        grid_spec=pltpu.PrefetchScalarGridSpec(
            num_scalar_prefetch=1,
            grid=(lead // take,),
            in_specs=[
                view(width),
                view(LANES),
                pl.BlockSpec((rows, LANES), lambda i, s: (0, 0)),
            ]
            + [whole] * 4,
            out_specs=[view(deep + LANES)] + [wide] * 6,
        ),
        out_shape=[jax.ShapeDtypeStruct((lead, rows, deep + LANES), BF)]
        + [jax.ShapeDtypeStruct((lead * rows, COLS), BF)] * 6,
        compiler_params=params(),
    )(spots, acts, meta, route, *mats)


def finish(parts_ref, token_ref, route_ref):
    deep = token_ref.shape[1]
    total = jnp.sum(parts_ref[...].astype(F32), axis=0)
    token_ref[...] = total[:, :deep].astype(BF)
    route = total[:, deep:]

    @pl.when(pl.program_id(0) == 0)
    def _():
        route_ref[...] = route

    @pl.when(pl.program_id(0) > 0)
    def _():
        route_ref[...] = route_ref[...] + route


def finish_call(parts, deep):
    _, rows, width = parts.shape
    return pl.pallas_call(
        finish,
        grid=(SIDE,),
        in_specs=[pl.BlockSpec((16, rows, width), lambda i: (i, 0, 0))],
        out_specs=[
            pl.BlockSpec((rows, deep), lambda i: (0, i)),
            pl.BlockSpec((rows, LANES), lambda i: (0, 0)),
        ],
        out_shape=[
            jax.ShapeDtypeStruct((rows, deep * SIDE), BF),
            jax.ShapeDtypeStruct((rows, LANES), F32),
        ],
        compiler_params=params(),
    )(parts)


def place(z, x, core):
    return (z % SIDE) * 8 + (x % SIDE) * 2 + core


def shift(arr, stage, by):
    pairs = []
    for z in range(SIDE):
        for x in range(SIDE):
            for core in range(2):
                along_x = core == stage
                goal = place(z, x + by, core) if along_x else place(z + by, x, core)
                pairs.append((place(z, x, core), goal))
    return lax.ppermute(arr, PLANE, pairs)


def swap(arr):
    return lax.ppermute(arr, "core", [(0, 1), (1, 0)])


def contract_rows(left, right):
    return lax.dot_general(left, right, (((0,), (0,)), ((), ())), preferred_element_type=F32)


def local(tokens, cotangent, routing, route_gates, gate_weight, up_weight, down_weight):
    tok_rows, full = tokens.shape
    width = gate_weight.shape[2]
    own_mats = [w.reshape(COLS, width) for w in (gate_weight, up_weight, down_weight)]
    mats = own_mats + [swap(w) for w in own_mats]
    meta = jnp.concatenate([routing.astype(BF), route_gates], axis=1)
    meta = jnp.pad(meta, ((0, 0), (0, LANES - meta.shape[1])))
    cut = lambda a: jnp.swapaxes(a.reshape(tok_rows, SIDE, width), 0, 1)
    meta_all = jnp.broadcast_to(meta[None], (SIDE, tok_rows, LANES))
    send = jnp.concatenate([cut(tokens), meta_all, cut(cotangent)], axis=2)
    own = lax.all_to_all(send, "ep", 0, 0, tiled=True)
    near = [own] + [shift(own, 0, s) for s in range(1, SIDE)]
    lap = width + LANES
    x_0 = jnp.concatenate([p[:, :, :lap] for p in near], axis=1)
    y_0 = jnp.concatenate([p[:, :, lap:] for p in near], axis=1)
    x_1, x_3 = shift(x_0, 1, 1), shift(x_0, 1, 3)
    y_1, y_3 = shift(y_0, 1, 1), shift(y_0, 1, 3)
    x_2, y_2 = shift(x_1, 1, 1), shift(y_3, 1, 3)
    pre_0 = pre_call([x_0], [y_0], mats)
    pre_13 = pre_call([x_1, x_3], [y_1, y_3], mats)
    pre_2 = pre_call([x_2], [y_2], mats)
    pre = jnp.concatenate([pre_0, pre_13, pre_2], axis=1)
    parts = lax.all_to_all(pre, "ep", 0, 0, tiled=True)
    stack = lambda ps: jnp.concatenate(ps, axis=1)
    meta_rows = stack([p[:, :, width:] for p in (x_0, x_1, x_3, x_2)])
    plane = lax.axis_index("ep").astype(jnp.int32)
    done, route = middle_call(plane.reshape(1), parts, meta_rows)
    acts = lax.all_gather(done[None], "ep", axis=0, tiled=True)
    z, x, core = (lax.axis_index(a).astype(jnp.int32) for a in PLANE)
    far = jnp.repeat(jnp.array([0, 1, 3, 2], jnp.int32), SIDE)
    close = jnp.tile(jnp.arange(SIDE, dtype=jnp.int32), SIDE)
    by_z = jnp.where(core == 0, far, close)
    by_x = jnp.where(core == 0, close, far)
    spots = ((z - by_z) % SIDE) * SIDE + (x - by_x) % SIDE
    spots = jnp.concatenate([spots, plane.reshape(1)])
    sent, *wides = terms_call(
        spots, acts, meta_rows, route, [mats[0], mats[1], mats[3], mats[4]]
    )
    got = lax.all_to_all(sent.reshape(-1, tok_rows, lap), TORUS, 0, 0, tiled=True)
    token_grad, route_sum = finish_call(got, width)
    route_grad = route_sum[:, :routing.shape[1]]
    x_rows = stack([p[:, :, :width] for p in (x_0, x_1, x_3, x_2)]).reshape(-1, width)
    y_rows = stack([y_0, y_1, y_3, y_2]).reshape(-1, width)
    grads = []
    for m in range(3):
        rows = y_rows if m == 2 else x_rows
        theirs = swap(contract_rows(wides[3 + m], rows).astype(BF))
        mine = contract_rows(wides[m], rows) + theirs.astype(F32)
        grads.append(mine.astype(BF).reshape(gate_weight.shape))
    return (token_grad, route_grad, *grads)


def solution(mesh):
    names = ("ep", "z", "x", "core")
    fine = Mesh(mesh.devices.reshape(SIDE, SIDE, SIDE, 2), names)
    rows = P(names, None)
    mats = P(None, PLANE, "ep")
    return jax.shard_map(
        local,
        mesh=fine,
        in_specs=(rows, rows, rows, rows, mats, mats, mats),
        out_specs=(rows, rows, mats, mats, mats),
        check_vma=False,
    )
```

```python
import jax
import jax.numpy as jnp
from jax import lax
from jax.experimental import pallas as pl
from jax.experimental.pallas import tpu as pltpu
from jax.sharding import Mesh
from jax.sharding import PartitionSpec as P

BF = jnp.bfloat16
F32 = jnp.float32
EXPERTS = 8
HID = 64
COLS = EXPERTS * HID
LANES = 128
SIDE = 4
PLANE = ("z", "x", "core")
TORUS = ("ep", "z", "x")


def params():
    return pltpu.CompilerParams(vmem_limit_bytes=58 << 20)


def first_half(rows):
    return lax.broadcasted_iota(jnp.int32, (rows, LANES), 1) < HID


def dot_t(rows, mat):
    return lax.dot_general(rows, mat, (((1,), (1,)), ((), ())), preferred_element_type=F32)


def flat(ref):
    lead, rows, width = ref.shape
    return ref[...].reshape(lead * rows, width)


def pre_acts(count, width):
    def body(*refs):
        xs, ys, mats = refs[:count], refs[count:2 * count], refs[2 * count:2 * count + 6]
        out_ref, acc_ref = refs[-2:]
        step = pl.program_id(0)
        chunk = mats[0].shape[0]
        x_all = jnp.concatenate([flat(r) for r in xs], axis=0)
        y = jnp.concatenate([flat(r) for r in ys], axis=0)
        rows = y.shape[0]
        x, meta = x_all[:, :width], x_all[:, width:].astype(F32)
        lane = lax.broadcasted_iota(jnp.int32, (rows, chunk), 1)
        owner = (lane // HID + step * (chunk // HID)).astype(F32)
        hit_a, hit_b = owner == meta[:, 0:1], owner == meta[:, 1:2]
        low = first_half(rows)
        lead, short_rows = xs[0].shape[0], xs[0].shape[1]
        for m in range(6):
            full = dot_t(y if m % 3 == 2 else x, mats[m][...])
            sums = []
            for k, hit in enumerate((hit_a, hit_b)):
                kept = jnp.where(hit, full, 0.0)
                short = sum(kept[:, g * LANES:(g + 1) * LANES] for g in range(chunk // LANES))
                spot = slice((2 * m + k) * LANES, (2 * m + k + 1) * LANES)
                short = short + jnp.where(step == 0, 0.0, acc_ref[:, spot])
                acc_ref[:, spot] = short
                sums.append(short + pltpu.roll(short, HID, 1))
            val = jnp.where(low, sums[0], sums[1]).astype(BF)
            for n in range(count):
                part = val[n * lead * short_rows:(n + 1) * lead * short_rows]
                part = part.reshape(lead, short_rows, LANES)
                out_ref[:, n * short_rows:(n + 1) * short_rows, m * LANES:(m + 1) * LANES] = part

    return body


def pre_call(xs, ys, mats, first, total, into):
    count = len(xs)
    lead, rows, _ = xs[0].shape
    width = ys[0].shape[2]
    steps = 2
    whole = lambda a: pl.BlockSpec(a.shape, lambda i: (0,) * a.ndim)
    extra = [] if into is None else [into]
    return pl.pallas_call(
        pre_acts(count, width),
        grid=(steps,),
        in_specs=[whole(a) for a in xs + ys]
        + [pl.BlockSpec((COLS // steps, width), lambda i: (i, 0))] * 6
        + [pl.BlockSpec(memory_space=pl.ANY)] * len(extra),
        out_specs=pl.BlockSpec((lead, rows * count, 6 * LANES), lambda i: (0, first // count, 0)),
        out_shape=jax.ShapeDtypeStruct((lead, rows * total, 6 * LANES), BF),
        scratch_shapes=[pltpu.VMEM((count * lead * rows, 12 * LANES), F32)],
        input_output_aliases={2 * count + 6: 0} if extra else {},
        compiler_params=params(),
    )(*xs, *ys, *mats, *extra)


def middle(plane_ref, parts_ref, meta_ref, out_ref, route_ref):
    rows = parts_ref.shape[1]
    meta = meta_ref[...].reshape(rows, LANES).astype(F32)
    low = first_half(rows)
    factor = jnp.where(low, meta[:, 2:3], meta[:, 3:4])
    prod = jnp.zeros((rows, LANES), F32)
    for side in range(2):
        vals = []
        for m in range(3):
            at = (3 * side + m) * LANES
            vals.append(sum(parts_ref[j, :, at:at + LANES].astype(F32) for j in range(SIDE)))
        gate, upper, reverse = vals
        sigma = jax.nn.sigmoid(gate)
        act = gate * sigma
        hidden = (act * upper).astype(BF).astype(F32)
        back = factor * reverse
        d_gate = back * upper * sigma * (1.0 + gate * (1.0 - sigma))
        at = 3 * side * LANES
        for n, val in enumerate((d_gate, back * act, factor * hidden)):
            low_bits = val.astype(BF)
            for j in range(SIDE):
                out_ref[j, :, at + n * LANES:at + (n + 1) * LANES] = low_bits
        prod = prod + hidden * reverse
    term_a = jnp.sum(jnp.where(low, prod, 0.0), axis=1, keepdims=True)
    term_b = jnp.sum(jnp.where(low, 0.0, prod), axis=1, keepdims=True)
    lane = lax.broadcasted_iota(jnp.int32, (rows, LANES), 1)
    route_ref[...] = jnp.where(lane == 0, term_a, jnp.where(lane == 1, term_b, 0.0)).astype(BF)


def middle_call(plane, parts, meta):
    _, rows, width = parts.shape
    return pl.pallas_call(
        middle,
        grid_spec=pltpu.PrefetchScalarGridSpec(
            num_scalar_prefetch=1,
            grid=(1,),
            in_specs=[
                pl.BlockSpec(parts.shape, lambda i, s: (0, 0, 0)),
                pl.BlockSpec((1, rows, LANES), lambda i, s: (s[0], 0, 0)),
            ],
            out_specs=[
                pl.BlockSpec((SIDE, rows, width), lambda i, s: (0, 0, 0)),
                pl.BlockSpec((rows, LANES), lambda i, s: (0, 0)),
            ],
        ),
        out_shape=[
            jax.ShapeDtypeStruct((SIDE, rows, width), BF),
            jax.ShapeDtypeStruct((rows, LANES), BF),
        ],
        compiler_params=params(),
    )(plane, parts, meta)


def spread(short, route_a, route_b, owner, low):
    turned = pltpu.roll(short, HID, 1)
    val_a = jnp.where(low, short, turned)
    val_b = jnp.where(low, turned, short)
    groups = COLS // LANES
    wide_a = jnp.concatenate([val_a] * groups, axis=1)
    wide_b = jnp.concatenate([val_b] * groups, axis=1)
    return jnp.where(owner == route_a, wide_a, jnp.where(owner == route_b, wide_b, 0.0))


def dense(acts_ref, meta_ref, picks):
    meta = flat(meta_ref).astype(F32)
    acts = flat(acts_ref).astype(F32)
    rows = meta.shape[0]
    lane = lax.broadcasted_iota(jnp.int32, (rows, COLS), 1)
    owner, low = (lane // HID).astype(F32), first_half(rows)
    return [
        spread(
            acts[:, m * LANES:(m + 1) * LANES], meta[:, 0:1], meta[:, 1:2], owner, low
        ).astype(BF)
        for m in picks
    ]


def widen(acts_ref, meta_ref, *outs):
    for out, val in zip(outs, dense(acts_ref, meta_ref, range(6))):
        out[...] = val


def widen_call(acts, meta):
    lead, rows, width = acts.shape
    view = lambda w: pl.BlockSpec((1, rows, w), lambda i: (i, 0, 0))
    return pl.pallas_call(
        widen,
        grid=(lead,),
        in_specs=[view(width), view(LANES)],
        out_specs=[pl.BlockSpec((rows, COLS), lambda i: (i, 0))] * 6,
        out_shape=[jax.ShapeDtypeStruct((lead * rows, COLS), BF)] * 6,
        compiler_params=params(),
    )(acts, meta)


def terms(spots_ref, acts_ref, meta_ref, route_ref, *refs):
    mats, out_ref, wide_ref = refs[:4], refs[4], refs[5]
    lead, rows, _ = acts_ref.shape
    step = pl.program_id(0)
    chunk = mats[0].shape[1]

    @pl.when(step == 0)
    def _():
        for n, val in enumerate(dense(acts_ref, meta_ref, (0, 1, 3, 4))):
            wide_ref[:, n * COLS:(n + 1) * COLS] = val
        route = route_ref[...].astype(F32)
        deep = out_ref.shape[2] - LANES
        for j in range(lead):
            mine = jnp.where(j == spots_ref[16], 1.0, 0.0)
            for b in range(16):
                spot = pl.multiple_of(spots_ref[b] * 8, 8)
                out_ref[j, pl.ds(spot, 8), deep:] = (route[b * 8:b * 8 + 8] * mine).astype(BF)

    wide = wide_ref[...]
    mat = jnp.concatenate([m[...] for m in mats], axis=0)
    total = jnp.dot(wide, mat, preferred_element_type=F32)
    where = pl.ds(pl.multiple_of(step * chunk, LANES), chunk)
    for j in range(lead):
        for b in range(16):
            at = j * rows + b * 8
            spot = pl.multiple_of(spots_ref[b] * 8, 8)
            out_ref[j, pl.ds(spot, 8), where] = total[at:at + 8].astype(BF)


def terms_call(spots, acts, meta, route, mats):
    lead, rows, _ = acts.shape
    deep = mats[0].shape[1]
    chunk = 256
    whole = lambda a: pl.BlockSpec(a.shape, lambda i, s: (0,) * a.ndim)
    out = jax.ShapeDtypeStruct((lead, rows, deep + LANES), BF)
    return pl.pallas_call(
        terms,
        grid_spec=pltpu.PrefetchScalarGridSpec(
            num_scalar_prefetch=1,
            grid=(deep // chunk,),
            in_specs=[whole(acts), whole(meta), whole(route)]
            + [pl.BlockSpec((COLS, chunk), lambda i, s: (0, i))] * 4,
            out_specs=whole(out),
            scratch_shapes=[pltpu.VMEM((lead * rows, 4 * COLS), BF)],
        ),
        out_shape=out,
        compiler_params=params(),
    )(spots, acts, meta, route, *mats)


def finish(parts_ref, token_ref, route_ref):
    deep = token_ref.shape[1]
    total = jnp.sum(parts_ref[...].astype(F32), axis=0)
    token_ref[...] = total[:, :deep].astype(BF)
    route = total[:, deep:]

    @pl.when(pl.program_id(0) == 0)
    def _():
        route_ref[...] = route

    @pl.when(pl.program_id(0) > 0)
    def _():
        route_ref[...] = route_ref[...] + route


def finish_call(parts, deep):
    _, rows, width = parts.shape
    return pl.pallas_call(
        finish,
        grid=(SIDE,),
        in_specs=[pl.BlockSpec((16, rows, width), lambda i: (i, 0, 0))],
        out_specs=[
            pl.BlockSpec((rows, deep), lambda i: (0, i)),
            pl.BlockSpec((rows, LANES), lambda i: (0, 0)),
        ],
        out_shape=[
            jax.ShapeDtypeStruct((rows, deep * SIDE), BF),
            jax.ShapeDtypeStruct((rows, LANES), F32),
        ],
        compiler_params=params(),
    )(parts)


def place(z, x, core):
    return (z % SIDE) * 8 + (x % SIDE) * 2 + core


def shift(arr, stage, by):
    pairs = []
    for z in range(SIDE):
        for x in range(SIDE):
            for core in range(2):
                along_x = core == stage
                goal = place(z, x + by, core) if along_x else place(z + by, x, core)
                pairs.append((place(z, x, core), goal))
    return lax.ppermute(arr, PLANE, pairs)


def swap(arr):
    return lax.ppermute(arr, "core", [(0, 1), (1, 0)])


def contract_rows(left, right):
    return lax.dot_general(left, right, (((0,), (0,)), ((), ())), preferred_element_type=F32)


def local(tokens, cotangent, routing, route_gates, gate_weight, up_weight, down_weight):
    tok_rows, _ = tokens.shape
    width = gate_weight.shape[2]
    own_mats = [w.reshape(COLS, width) for w in (gate_weight, up_weight, down_weight)]
    mats = own_mats + [swap(w) for w in own_mats]
    meta = jnp.concatenate([routing.astype(BF), route_gates], axis=1)
    meta = jnp.pad(meta, ((0, 0), (0, LANES - meta.shape[1])))
    cut = lambda a: jnp.swapaxes(a.reshape(tok_rows, SIDE, width), 0, 1)
    meta_all = jnp.broadcast_to(meta[None], (SIDE, tok_rows, LANES))
    send = jnp.concatenate([cut(tokens), meta_all, cut(cotangent)], axis=2)
    own = lax.all_to_all(send, "ep", 0, 0, tiled=True)
    near = [own] + [shift(own, 0, s) for s in range(1, SIDE)]
    lap = width + LANES
    x_0 = jnp.concatenate([p[:, :, :lap] for p in near], axis=1)
    y_0 = jnp.concatenate([p[:, :, lap:] for p in near], axis=1)
    x_1, x_3 = shift(x_0, 1, 1), shift(x_0, 1, 3)
    y_1, y_3 = shift(y_0, 1, 1), shift(y_0, 1, 3)
    x_2, y_2 = shift(x_1, 1, 1), shift(y_3, 1, 3)
    early = pre_call([x_0, x_1, x_3], [y_0, y_1, y_3], mats, 0, SIDE, None)
    pre = pre_call([x_2], [y_2], mats, SIDE - 1, SIDE, early)
    parts = lax.all_to_all(pre, "ep", 0, 0, tiled=True)
    stack = lambda ps: jnp.concatenate(ps, axis=1)
    meta_rows = stack([p[:, :, width:] for p in (x_0, x_1, x_3, x_2)])
    plane = lax.axis_index("ep").astype(jnp.int32)
    done, route = middle_call(plane.reshape(1), parts, meta_rows)
    acts = lax.all_to_all(done, "ep", 0, 0, tiled=True)
    z, x, core = (lax.axis_index(a).astype(jnp.int32) for a in PLANE)
    far = jnp.repeat(jnp.array([0, 1, 3, 2], jnp.int32), SIDE)
    close = jnp.tile(jnp.arange(SIDE, dtype=jnp.int32), SIDE)
    by_z = jnp.where(core == 0, far, close)
    by_x = jnp.where(core == 0, close, far)
    spots = ((z - by_z) % SIDE) * SIDE + (x - by_x) % SIDE
    spots = jnp.concatenate([spots, plane.reshape(1)])
    sent = terms_call(spots, acts, meta_rows, route, [mats[0], mats[1], mats[3], mats[4]])
    got = lax.all_to_all(sent.reshape(-1, tok_rows, lap), TORUS, 0, 0, tiled=True)
    wides = widen_call(acts, meta_rows)
    token_grad, route_sum = finish_call(got, width)
    route_grad = route_sum[:, :routing.shape[1]]
    x_rows = stack([p[:, :, :width] for p in (x_0, x_1, x_3, x_2)]).reshape(-1, width)
    y_rows = stack([y_0, y_1, y_3, y_2]).reshape(-1, width)
    grads = []
    for m in range(3):
        rows = y_rows if m == 2 else x_rows
        theirs = swap(contract_rows(wides[3 + m], rows).astype(BF))
        mine = contract_rows(wides[m], rows) + theirs.astype(F32)
        grads.append(mine.astype(BF).reshape(gate_weight.shape))
    return (token_grad, route_grad, *grads)


def solution(mesh):
    names = ("ep", "z", "x", "core")
    fine = Mesh(mesh.devices.reshape(SIDE, SIDE, SIDE, 2), names)
    rows = P(names, None)
    mats = P(None, PLANE, "ep")

    return jax.shard_map(
        local,
        mesh=fine,
        in_specs=(rows, rows, rows, rows, mats, mats, mats),
        out_specs=(rows, rows, mats, mats, mats),
        check_vma=False,
    )
```

```python
import jax
import jax.numpy as jnp
from jax import lax
from jax.experimental import pallas as pl
from jax.experimental.pallas import tpu as pltpu
from jax.sharding import Mesh
from jax.sharding import PartitionSpec as P

BF = jnp.bfloat16
F32 = jnp.float32
EXPERTS = 8
HID = 64
COLS = EXPERTS * HID
LANES = 128
SIDE = 4
FAR = (1, 3, 0, 2)
PLANE = ("z", "x", "core")
TORUS = ("ep", "z", "x")


def params(mib):
    return pltpu.CompilerParams(vmem_limit_bytes=mib << 20)


def near_core(arr):
    return pltpu.with_memory_space_constraint(arr, pltpu.VMEM)


def far_off(arr):
    return pltpu.with_memory_space_constraint(arr, pltpu.HBM)


def in_core(count):
    return [pl.BlockSpec(memory_space=pltpu.VMEM)] * count


def first_half(rows):
    return lax.broadcasted_iota(jnp.int32, (rows, LANES), 1) < HID


def dot_t(rows, mat):
    return lax.dot_general(rows, mat, (((1,), (1,)), ((), ())), preferred_element_type=F32)


def flat(ref):
    lead, rows, width = ref.shape
    return ref[...].reshape(lead * rows, width)


def pack(tok_ref, cot_ref, route_ref, gates_ref, out_ref):
    rows, full = tok_ref.shape
    width = full // SIDE
    lap = width + LANES
    eye = lax.broadcasted_iota(jnp.int32, (rows, rows), 0) == lax.broadcasted_iota(
        jnp.int32, (rows, rows), 1
    )
    lane = lax.broadcasted_iota(jnp.int32, (rows, LANES), 1)
    meta = jnp.zeros((rows, LANES), F32)
    for n, ref in enumerate((route_ref, gates_ref)):
        vals = ref[...].astype(F32)
        for k in range(2):
            column = jnp.sum(jnp.where(eye, vals[k:k + 1, :], 0.0), axis=1, keepdims=True)
            meta = jnp.where(lane == 2 * n + k, column, meta)
    meta = meta.astype(BF)
    for j in range(SIDE):
        out_ref[j, :, :width] = tok_ref[:, j * width:(j + 1) * width]
        out_ref[j, :, width:lap] = meta
        out_ref[j, :, lap:] = cot_ref[:, j * width:(j + 1) * width]


def pack_call(tokens, cotangent, routing, gates, width):
    args = (tokens, cotangent, routing.T, gates.T)
    rows = tokens.shape[0]
    out = pltpu.HBM((SIDE, rows, 2 * width + LANES), BF)
    return pl.pallas_call(
        pack,
        grid=(1,),
        in_specs=[pl.BlockSpec(a.shape, lambda i: (0, 0)) for a in args],
        out_specs=pl.BlockSpec(out.shape, lambda i: (0, 0, 0)),
        out_shape=out,
        compiler_params=params(8),
    )(*map(far_off, args))


def load(*refs):
    count = len(refs) // 2
    mats, outs, sems = refs[:count], refs[count:2 * count], refs[-1]
    copies = [pltpu.make_async_copy(mats[m], outs[m], sems.at[m]) for m in range(count)]
    for copy in copies:
        copy.start()
    for copy in copies:
        copy.wait()


def load_call(mats):
    return pl.pallas_call(
        load,
        in_specs=[pl.BlockSpec(memory_space=pl.ANY)] * len(mats),
        out_specs=in_core(len(mats)),
        out_shape=[pltpu.VMEM(m.shape, BF) for m in mats],
        scratch_shapes=[pltpu.SemaphoreType.DMA((len(mats),))],
        compiler_params=params(2),
    )(*map(far_off, mats))


def stack(*refs):
    pieces, x_ref, y_ref = refs[:SIDE], refs[SIDE], refs[SIDE + 1]
    lap, rows = x_ref.shape[2], pieces[0].shape[1]
    for n, piece in enumerate(pieces):
        x_ref[:, n * rows:(n + 1) * rows, :] = piece[:, :, :lap]
        y_ref[:, n * rows:(n + 1) * rows, :] = piece[:, :, lap:]


def stack_call(pieces, lap):
    lead, rows, width = pieces[0].shape
    return pl.pallas_call(
        stack,
        in_specs=in_core(SIDE),
        out_specs=in_core(2),
        out_shape=[
            pltpu.VMEM((lead, SIDE * rows, lap), BF),
            pltpu.VMEM((lead, SIDE * rows, width - lap), BF),
        ],
        compiler_params=params(8),
    )(*map(near_core, pieces))


def pre_acts(count, first, width):
    def body(*refs):
        x_refs, y_refs, mats = refs[:count], refs[count:2 * count], refs[2 * count:2 * count + 6]
        out_ref, x_out, y_out, meta_out, sems = refs[-5:]
        lead, short_rows = x_refs[0].shape[0], x_refs[0].shape[1]
        copies = []
        for n in range(count):
            rows_at = pl.ds(first + n * short_rows, short_rows)
            jobs = (
                (x_refs[n].at[:, :, :width], x_out.at[:, rows_at, :]),
                (y_refs[n], y_out.at[:, rows_at, :]),
                (x_refs[n].at[:, :, width:], meta_out.at[:, rows_at, :]),
            )
            for k, (src, dst) in enumerate(jobs):
                copies.append(pltpu.make_async_copy(src, dst, sems.at[n, k]))
        for copy in copies:
            copy.start()
        x_all = jnp.concatenate([flat(r) for r in x_refs], axis=0)
        y = jnp.concatenate([flat(r) for r in y_refs], axis=0)
        rows = y.shape[0]
        x, meta = x_all[:, :width], x_all[:, width:].astype(F32)
        lane = lax.broadcasted_iota(jnp.int32, (rows, COLS), 1)
        owner = (lane // HID).astype(F32)
        hit_a, hit_b = owner == meta[:, 0:1], owner == meta[:, 1:2]
        low = first_half(rows)
        for m in range(6):
            full = dot_t(y if m % 3 == 2 else x, mats[m][...])
            sums = []
            for hit in (hit_a, hit_b):
                kept = jnp.where(hit, full, 0.0)
                short = sum(kept[:, g * LANES:(g + 1) * LANES] for g in range(COLS // LANES))
                sums.append(short + pltpu.roll(short, HID, 1))
            val = jnp.where(low, sums[0], sums[1]).astype(BF)
            for n in range(count):
                part = val[n * lead * short_rows:(n + 1) * lead * short_rows]
                part = part.reshape(lead, short_rows, LANES)
                out_ref[:, n * short_rows:(n + 1) * short_rows, m * LANES:(m + 1) * LANES] = part
        for copy in copies:
            copy.wait()

    return body


def pre_call(pieces, mats, first, total, into):
    count = len(pieces) // 2
    lead, rows, _ = pieces[0].shape
    width = mats[0].shape[1]
    outer = pl.BlockSpec(memory_space=pl.ANY)
    outs = [pltpu.HBM((lead, rows * total, w), BF) for w in (6 * LANES, width, width, LANES)]
    taken = len(pieces) + 6
    return pl.pallas_call(
        pre_acts(count, first * rows, width),
        grid=(1,),
        in_specs=in_core(taken) + [outer] * len(into),
        out_specs=[
            pl.BlockSpec((lead, rows * count, 6 * LANES), lambda i: (0, first // count, 0)),
            outer,
            outer,
            outer,
        ],
        out_shape=outs,
        scratch_shapes=[pltpu.SemaphoreType.DMA((count, 3))],
        input_output_aliases={taken + n: n for n in range(len(into))},
        compiler_params=params(12),
    )(*map(near_core, pieces), *map(near_core, mats), *map(far_off, into))


def middle(plane_ref, parts_ref, meta_ref, out_ref, route_ref):
    rows = parts_ref.shape[1]
    meta = meta_ref[...].reshape(rows, LANES).astype(F32)
    low = first_half(rows)
    factor = jnp.where(low, meta[:, 2:3], meta[:, 3:4])
    prod = jnp.zeros((rows, LANES), F32)
    for side in range(2):
        vals = []
        for m in range(3):
            at = (3 * side + m) * LANES
            vals.append(sum(parts_ref[j, :, at:at + LANES].astype(F32) for j in range(SIDE)))
        gate, upper, reverse = vals
        sigma = jax.nn.sigmoid(gate)
        act = gate * sigma
        hidden = (act * upper).astype(BF).astype(F32)
        back = factor * reverse
        d_gate = back * upper * sigma * (1.0 + gate * (1.0 - sigma))
        at = 3 * side * LANES
        for n, val in enumerate((d_gate, back * act, factor * hidden)):
            low_bits = val.astype(BF)
            for j in range(SIDE):
                out_ref[j, :, at + n * LANES:at + (n + 1) * LANES] = low_bits
        prod = prod + hidden * reverse
    term_a = jnp.sum(jnp.where(low, prod, 0.0), axis=1, keepdims=True)
    term_b = jnp.sum(jnp.where(low, 0.0, prod), axis=1, keepdims=True)
    lane = lax.broadcasted_iota(jnp.int32, (rows, LANES), 1)
    route_ref[...] = jnp.where(lane == 0, term_a, jnp.where(lane == 1, term_b, 0.0)).astype(BF)


def middle_call(plane, parts, meta):
    _, rows, width = parts.shape
    return pl.pallas_call(
        middle,
        grid_spec=pltpu.PrefetchScalarGridSpec(
            num_scalar_prefetch=1,
            grid=(1,),
            in_specs=[
                pl.BlockSpec(memory_space=pltpu.VMEM),
                pl.BlockSpec((1, rows, LANES), lambda i, s: (s[0], 0, 0)),
            ],
            out_specs=[
                pl.BlockSpec((SIDE, rows, width), lambda i, s: (0, 0, 0)),
                pl.BlockSpec((rows, LANES), lambda i, s: (0, 0)),
            ],
        ),
        out_shape=[
            pltpu.HBM((SIDE, rows, width), BF),
            jax.ShapeDtypeStruct((rows, LANES), BF),
        ],
        compiler_params=params(16),
    )(plane, near_core(parts), meta)


def spread(short, route_a, route_b, owner, low):
    turned = pltpu.roll(short, HID, 1)
    val_a = jnp.where(low, short, turned)
    val_b = jnp.where(low, turned, short)
    groups = COLS // LANES
    wide_a = jnp.concatenate([val_a] * groups, axis=1)
    wide_b = jnp.concatenate([val_b] * groups, axis=1)
    return jnp.where(owner == route_a, wide_a, jnp.where(owner == route_b, wide_b, 0.0))


def dense(acts, meta, picks):
    rows = meta.shape[0]
    lane = lax.broadcasted_iota(jnp.int32, (rows, COLS), 1)
    owner, low = (lane // HID).astype(F32), first_half(rows)
    return [
        spread(
            acts[:, m * LANES:(m + 1) * LANES], meta[:, 0:1], meta[:, 1:2], owner, low
        ).astype(BF)
        for m in picks
    ]


def widen(acts_ref, meta_ref, *outs):
    for out, val in zip(outs, dense(flat(acts_ref).astype(F32), flat(meta_ref).astype(F32), range(6))):
        out[...] = val


def widen_call(acts, meta):
    lead, rows, _ = acts.shape
    return pl.pallas_call(
        widen,
        in_specs=in_core(2),
        out_specs=in_core(6),
        out_shape=[pltpu.VMEM((lead * rows, COLS), BF)] * 6,
        compiler_params=params(8),
    )(near_core(acts), near_core(meta))


def goals(z, x, core):
    spots = []
    for b in range(16):
        far, close = FAR[b // SIDE], b % SIDE
        by_z = jnp.where(core == 0, far, close)
        by_x = jnp.where(core == 0, close, far)
        spots.append(((z - by_z) & 3) * SIDE + ((x - by_x) & 3))
    return spots


def terms(plane_ref, z_ref, x_ref, core_ref, acts_ref, meta_ref, route_ref, *refs):
    mats, sent_ref, wide_ref, out_ref, sort_ref, out_sems = refs[:4], *refs[4:]
    lead, rows, _ = acts_ref.shape
    deep = out_ref.shape[2] - LANES
    chunk = 256
    count = deep // chunk
    cuts = [slice(c * chunk, (c + 1) * chunk) for c in range(count)] + [slice(deep, deep + LANES)]
    stores = [
        pltpu.make_async_copy(out_ref.at[:, :, cut], sent_ref.at[:, :, cut], out_sems.at[c])
        for c, cut in enumerate(cuts)
    ]
    acts, meta = flat(acts_ref).astype(F32), flat(meta_ref).astype(F32)
    route = route_ref[...].astype(F32)
    width = acts.shape[1]
    spots = goals(z_ref[0], x_ref[0], core_ref[0])
    for j in range(lead):
        mine = jnp.where(j == plane_ref[0], 1.0, 0.0)
        for b in range(16):
            at = j * rows + b * 8
            spot = pl.ds(pl.multiple_of(j * rows + spots[b] * 8, 8), 8)
            sort_ref[spot, :width] = acts[at:at + 8]
            sort_ref[spot, width:width + LANES] = meta[at:at + 8]
            sort_ref[spot, width + LANES:] = route[b * 8:b * 8 + 8] * mine
    moved = sort_ref[:, :width], sort_ref[:, width:width + LANES]
    for n, val in enumerate(dense(*moved, (0, 1, 3, 4))):
        wide_ref[:, n * COLS:(n + 1) * COLS] = val
    out_ref[:, :, cuts[-1]] = sort_ref[:, width + LANES:].astype(BF).reshape(lead, rows, LANES)
    stores[-1].start()
    for c in range(count):
        mat = jnp.concatenate([m[:, cuts[c]] for m in mats], axis=0)
        total = jnp.dot(wide_ref[...], mat, preferred_element_type=F32)
        out_ref[:, :, cuts[c]] = total.astype(BF).reshape(lead, rows, chunk)
        stores[c].start()
    for copy in stores:
        copy.wait()


def terms_call(spots, acts, meta, route, mats):
    lead, rows, _ = acts.shape
    deep = mats[0].shape[1]
    out = (lead, rows, deep + LANES)
    chunk = 256
    outer = pl.BlockSpec(memory_space=pl.ANY)
    return pl.pallas_call(
        terms,
        grid_spec=pltpu.PrefetchScalarGridSpec(
            num_scalar_prefetch=4,
            grid=(1,),
            in_specs=in_core(7),
            out_specs=outer,
            scratch_shapes=[
                pltpu.VMEM((lead * rows, 4 * COLS), BF),
                pltpu.VMEM(out, BF),
                pltpu.VMEM((lead * rows, 8 * LANES), F32),
                pltpu.SemaphoreType.DMA((deep // chunk + 1,)),
            ],
        ),
        out_shape=pltpu.HBM(out, BF),
        compiler_params=params(16),
    )(*spots, *map(near_core, (acts, meta, route, *mats)))


def finish(parts_ref, token_ref, route_ref):
    rows, width = parts_ref.shape[1:]
    deep = width - LANES
    group = parts_ref.shape[0] // SIDE
    route = jnp.zeros((rows, LANES), F32)
    for j in range(SIDE):
        total = jnp.zeros((rows, width), F32)
        for n in range(group):
            total = total + parts_ref[j * group + n].astype(F32)
        token_ref[:, j * deep:(j + 1) * deep] = total[:, :deep].astype(BF)
        route = route + total[:, deep:]
    eye = lax.broadcasted_iota(jnp.int32, (rows, rows), 0) == lax.broadcasted_iota(
        jnp.int32, (rows, rows), 1
    )
    for k in range(2):
        column = route[:, k:k + 1]
        route_ref[k:k + 1, :] = jnp.sum(jnp.where(eye, column, 0.0), axis=0, keepdims=True)


def finish_call(parts, deep):
    _, rows, _ = parts.shape
    return pl.pallas_call(
        finish,
        in_specs=in_core(1),
        out_shape=[
            jax.ShapeDtypeStruct((rows, deep * SIDE), BF),
            jax.ShapeDtypeStruct((2, rows), F32),
        ],
        compiler_params=params(8),
    )(near_core(parts))


def place(z, x, core):
    return (z % SIDE) * 8 + (x % SIDE) * 2 + core


def shift(arr, stage, by):
    pairs = []
    for z in range(SIDE):
        for x in range(SIDE):
            for core in range(2):
                along_x = core == stage
                goal = place(z, x + by, core) if along_x else place(z + by, x, core)
                pairs.append((place(z, x, core), goal))
    return lax.ppermute(arr, PLANE, pairs)


def swap(arr):
    return lax.ppermute(arr, "core", [(0, 1), (1, 0)])


def contract_rows(left, right):
    return lax.dot_general(left, right, (((0,), (0,)), ((), ())), preferred_element_type=F32)


def local(tokens, cotangent, routing, route_gates, gate_weight, up_weight, down_weight):
    tok_rows, _ = tokens.shape
    width = gate_weight.shape[2]
    own_mats = [w.reshape(COLS, width) for w in (gate_weight, up_weight, down_weight)]
    their_mats = [swap(w) for w in own_mats]
    mats = load_call(own_mats + their_mats)
    send = pack_call(tokens, cotangent, routing, route_gates, width)
    own = lax.all_to_all(send, "ep", 0, 0, tiled=True)
    near = [own] + [shift(own, 0, s) for s in range(1, SIDE)]
    lap = width + LANES
    x_0, y_0 = stack_call(near, lap)
    x_1 = shift(x_0, 1, 1)
    y_3 = shift(y_0, 1, 3)
    x_3 = shift(x_0, 1, 3)
    y_1 = shift(y_0, 1, 1)
    x_2 = shift(x_1, 1, 1)
    y_2 = shift(y_3, 1, 3)
    plane, *spot = (
        lax.axis_index(a).astype(jnp.int32).reshape(1) for a in ("ep",) + PLANE
    )
    state = pre_call([x_0, y_0], mats, 2, SIDE, [])
    state = pre_call([x_1, x_3, y_1, y_3], mats, 0, SIDE, state)
    pre, x_rows, y_rows, meta_rows = pre_call([x_2, y_2], mats, 3, SIDE, state)
    parts = lax.all_to_all(pre, "ep", 0, 0, tiled=True)
    done, route = middle_call(plane, parts, meta_rows)
    acts = lax.all_to_all(done, "ep", 0, 0, tiled=True)
    sent = terms_call((plane, *spot), acts, meta_rows, route, mats[:2] + mats[3:5])
    got = lax.all_to_all(sent.reshape(-1, tok_rows, lap), TORUS, 0, 0, tiled=True)
    wides = widen_call(acts, meta_rows)
    token_grad, route_sum = finish_call(got, width)
    route_grad = route_sum.T
    x_rows, y_rows = (r.reshape(-1, width) for r in (x_rows, y_rows))
    grads = []
    for m in range(3):
        rows = y_rows if m == 2 else x_rows
        theirs = swap(contract_rows(wides[3 + m], rows).astype(BF))
        mine = contract_rows(wides[m], rows) + theirs.astype(F32)
        grads.append(mine.astype(BF).reshape(gate_weight.shape))
    return (token_grad, route_grad, *grads)


def solution(mesh):
    names = ("ep", "z", "x", "core")
    fine = Mesh(mesh.devices.reshape(SIDE, SIDE, SIDE, 2), names)
    rows = P(names, None)
    mats = P(None, PLANE, "ep")

    return jax.shard_map(
        local,
        mesh=fine,
        in_specs=(rows, rows, rows, rows, mats, mats, mats),
        out_specs=(rows, rows, mats, mats, mats),
        check_vma=False,
    )
```

```python
import jax
import jax.numpy as jnp
from jax import lax
from jax.experimental import pallas as pl
from jax.experimental.pallas import tpu as pltpu
from jax.sharding import Mesh
from jax.sharding import PartitionSpec as P

BF = jnp.bfloat16
F32 = jnp.float32
EXPERTS = 8
HID = 64
COLS = EXPERTS * HID
LANES = 128
SIDE = 4
FAR = (1, 3, 0, 2)
PLANE = ("z", "x", "core")
TORUS = ("ep", "z", "x")


def params(mib):
    return pltpu.CompilerParams(vmem_limit_bytes=mib << 20)


def near_core(arr):
    return pltpu.with_memory_space_constraint(arr, pltpu.VMEM)


def far_off(arr):
    return pltpu.with_memory_space_constraint(arr, pltpu.HBM)


def in_core(count):
    return [pl.BlockSpec(memory_space=pltpu.VMEM)] * count


def first_half(rows):
    return lax.broadcasted_iota(jnp.int32, (rows, LANES), 1) < HID


def dot_t(rows, mat):
    return lax.dot_general(rows, mat, (((1,), (1,)), ((), ())), preferred_element_type=F32)


def flat(ref):
    lead, rows, width = ref.shape
    return ref[...].reshape(lead * rows, width)


def pack(plane_ref, z_ref, chip_ref, core_ref, tok_ref, cot_ref, route_ref, gates_ref, out_ref):
    rows, full = tok_ref.shape
    width = full // SIDE
    lap = width + LANES
    eye = lax.broadcasted_iota(jnp.int32, (rows, rows), 0) == lax.broadcasted_iota(
        jnp.int32, (rows, rows), 1
    )
    lane = lax.broadcasted_iota(jnp.int32, (rows, LANES), 1)
    meta = jnp.zeros((rows, LANES), F32)
    for n, ref in enumerate((route_ref, gates_ref)):
        vals = ref[...].astype(F32)
        for k in range(2):
            column = jnp.sum(jnp.where(eye, vals[k:k + 1, :], 0.0), axis=1, keepdims=True)
            meta = jnp.where(lane == 2 * n + k, column, meta)
    meta = meta.astype(BF)
    for j in range(SIDE):
        out_ref[j, :, :width] = tok_ref[:, j * width:(j + 1) * width]
        out_ref[j, :, width:lap] = meta
        out_ref[j, :, lap:] = cot_ref[:, j * width:(j + 1) * width]


def pack_call(spot, tokens, cotangent, routing, gates, width):
    args = (tokens, cotangent, routing.T, gates.T)
    rows = tokens.shape[0]
    out = pltpu.HBM((SIDE, rows, 2 * width + LANES), BF)
    return pl.pallas_call(
        pack,
        grid_spec=pltpu.PrefetchScalarGridSpec(
            num_scalar_prefetch=4,
            grid=(1,),
            in_specs=[pl.BlockSpec(a.shape, lambda i, *s: (0, 0)) for a in args],
            out_specs=pl.BlockSpec(out.shape, lambda i, *s: (0, 0, 0)),
        ),
        out_shape=out,
        compiler_params=params(8),
    )(*spot, *map(far_off, args))


def load(*refs):
    count = len(refs) // 2
    mats, outs, sems = refs[:count], refs[count:2 * count], refs[-1]
    copies = [pltpu.make_async_copy(mats[m], outs[m], sems.at[m]) for m in range(count)]
    for copy in copies:
        copy.start()
    for copy in copies:
        copy.wait()


def load_call(mats):
    return pl.pallas_call(
        load,
        in_specs=[pl.BlockSpec(memory_space=pl.ANY)] * len(mats),
        out_specs=in_core(len(mats)),
        out_shape=[pltpu.VMEM(m.shape, BF) for m in mats],
        scratch_shapes=[pltpu.SemaphoreType.DMA((len(mats),))],
        compiler_params=params(2),
    )(*map(far_off, mats))


def stack(*refs):
    pieces, x_ref, y_ref = refs[:SIDE], refs[SIDE], refs[SIDE + 1]
    lap, rows = x_ref.shape[2], pieces[0].shape[1]
    for n, piece in enumerate(pieces):
        x_ref[:, n * rows:(n + 1) * rows, :] = piece[:, :, :lap]
        y_ref[:, n * rows:(n + 1) * rows, :] = piece[:, :, lap:]


def stack_call(pieces, lap):
    lead, rows, width = pieces[0].shape
    return pl.pallas_call(
        stack,
        in_specs=in_core(SIDE),
        out_specs=in_core(2),
        out_shape=[
            pltpu.VMEM((lead, SIDE * rows, lap), BF),
            pltpu.VMEM((lead, SIDE * rows, width - lap), BF),
        ],
        compiler_params=params(8),
    )(*map(near_core, pieces))


def pre_acts(count, first, width):
    def body(plane_ref, *refs):
        x_refs, y_refs, mats = refs[:count], refs[count:2 * count], refs[2 * count:2 * count + 6]
        *outs, x_out, y_out, meta_out, val_ref, sems, out_sems = refs[-10:]
        lead, short_rows = x_refs[0].shape[0], x_refs[0].shape[1]
        copies = []
        for n in range(count):
            rows_at = pl.ds(first + n * short_rows, short_rows)
            jobs = (
                (x_refs[n].at[:, :, :width], x_out.at[:, rows_at, :]),
                (y_refs[n], y_out.at[:, rows_at, :]),
                (x_refs[n].at[:, :, width:], meta_out.at[:, rows_at, :]),
            )
            for k, (src, dst) in enumerate(jobs):
                copies.append(pltpu.make_async_copy(src, dst, sems.at[n, k]))
        for copy in copies:
            copy.start()
        x_all = jnp.concatenate([flat(r) for r in x_refs], axis=0)
        y = jnp.concatenate([flat(r) for r in y_refs], axis=0)
        rows = y.shape[0]
        x, meta = x_all[:, :width], x_all[:, width:].astype(F32)
        lane = lax.broadcasted_iota(jnp.int32, (rows, COLS), 1)
        owner = (lane // HID).astype(F32)
        hit_a, hit_b = owner == meta[:, 0:1], owner == meta[:, 1:2]
        low = first_half(rows)
        for m in range(6):
            full = dot_t(y if m % 3 == 2 else x, mats[m][...])
            sums = []
            for hit in (hit_a, hit_b):
                kept = jnp.where(hit, full, 0.0)
                short = sum(kept[:, g * LANES:(g + 1) * LANES] for g in range(COLS // LANES))
                sums.append(short + pltpu.roll(short, HID, 1))
            val = jnp.where(low, sums[0], sums[1]).astype(BF)
            for n in range(count):
                part = val[n * lead * short_rows:(n + 1) * lead * short_rows]
                part = part.reshape(lead, short_rows, LANES)
                val_ref[:, n * short_rows:(n + 1) * short_rows, m * LANES:(m + 1) * LANES] = part
        for k in range(lead):
            copy = pltpu.make_async_copy(
                val_ref.at[(plane_ref[0] + k) & 3],
                outs[k].at[pl.ds(first, count * short_rows), :],
                out_sems.at[k],
            )
            copy.start()
            copies.append(copy)
        for copy in copies:
            copy.wait()

    return body


def pre_call(plane, pieces, mats, first, total, into):
    count = len(pieces) // 2
    lead, rows, _ = pieces[0].shape
    width = mats[0].shape[1]
    outer = pl.BlockSpec(memory_space=pl.ANY)
    outs = [pltpu.HBM((rows * total, 6 * LANES), BF)] * lead
    outs = outs + [pltpu.HBM((lead, rows * total, w), BF) for w in (width, width, LANES)]
    taken = len(pieces) + 6
    return pl.pallas_call(
        pre_acts(count, first * rows, width),
        grid_spec=pltpu.PrefetchScalarGridSpec(
            num_scalar_prefetch=1,
            grid=(1,),
            in_specs=in_core(taken) + [outer] * len(into),
            out_specs=[outer] * len(outs),
            scratch_shapes=[
                pltpu.VMEM((lead, rows * count, 6 * LANES), BF),
                pltpu.SemaphoreType.DMA((count, 3)),
                pltpu.SemaphoreType.DMA((lead,)),
            ],
        ),
        out_shape=outs,
        input_output_aliases={1 + taken + n: n for n in range(len(into))},
        compiler_params=params(14),
    )(plane, *map(near_core, pieces), *map(near_core, mats), *map(far_off, into))


def middle(plane_ref, *refs):
    parts, meta_ref, out_ref, route_ref = refs[:SIDE], *refs[SIDE:]
    rows = out_ref.shape[0]
    meta = meta_ref[...].reshape(rows, LANES).astype(F32)
    low = first_half(rows)
    factor = jnp.where(low, meta[:, 2:3], meta[:, 3:4])
    prod = jnp.zeros((rows, LANES), F32)
    for side in range(2):
        vals = []
        for m in range(3):
            at = (3 * side + m) * LANES
            vals.append(sum(part[:, at:at + LANES].astype(F32) for part in parts))
        gate, upper, reverse = vals
        sigma = jax.nn.sigmoid(gate)
        act = gate * sigma
        hidden = (act * upper).astype(BF).astype(F32)
        back = factor * reverse
        d_gate = back * upper * sigma * (1.0 + gate * (1.0 - sigma))
        at = 3 * side * LANES
        for n, val in enumerate((d_gate, back * act, factor * hidden)):
            out_ref[:, at + n * LANES:at + (n + 1) * LANES] = val.astype(BF)
        prod = prod + hidden * reverse
    term_a = jnp.sum(jnp.where(low, prod, 0.0), axis=1, keepdims=True)
    term_b = jnp.sum(jnp.where(low, 0.0, prod), axis=1, keepdims=True)
    lane = lax.broadcasted_iota(jnp.int32, (rows, LANES), 1)
    route_ref[...] = jnp.where(lane == 0, term_a, jnp.where(lane == 1, term_b, 0.0)).astype(BF)


def middle_call(plane, parts, meta):
    rows, width = parts[0].shape
    return pl.pallas_call(
        middle,
        grid_spec=pltpu.PrefetchScalarGridSpec(
            num_scalar_prefetch=1,
            grid=(1,),
            in_specs=[pl.BlockSpec((rows, width), lambda i, s: (0, 0))]
            + in_core(SIDE - 1)
            + [pl.BlockSpec((1, rows, LANES), lambda i, s: (s[0], 0, 0))],
            out_specs=in_core(2),
        ),
        out_shape=[pltpu.VMEM((rows, width), BF), pltpu.VMEM((rows, LANES), BF)],
        compiler_params=params(6),
    )(plane, far_off(parts[0]), *map(near_core, parts[1:]), far_off(meta))


def spread(short, route_a, route_b, owner, low):
    turned = pltpu.roll(short, HID, 1)
    val_a = jnp.where(low, short, turned)
    val_b = jnp.where(low, turned, short)
    groups = COLS // LANES
    wide_a = jnp.concatenate([val_a] * groups, axis=1)
    wide_b = jnp.concatenate([val_b] * groups, axis=1)
    return jnp.where(owner == route_a, wide_a, jnp.where(owner == route_b, wide_b, 0.0))


def dense(acts, meta, picks):
    rows = meta.shape[0]
    lane = lax.broadcasted_iota(jnp.int32, (rows, COLS), 1)
    owner, low = (lane // HID).astype(F32), first_half(rows)
    return [
        spread(
            acts[:, m * LANES:(m + 1) * LANES], meta[:, 0:1], meta[:, 1:2], owner, low
        ).astype(BF)
        for m in picks
    ]


def widen(plane_ref, *refs):
    acts, meta_ref, outs = refs[:SIDE], refs[SIDE], refs[SIDE + 1:]
    rows = acts[0].shape[0]
    for k, ref in enumerate(acts):
        home = (plane_ref[0] - k) & 3
        vals = dense(ref[...].astype(F32), meta_ref[home].astype(F32), range(6))
        for out, val in zip(outs, vals):
            out[pl.ds(pl.multiple_of(home * rows, rows), rows), :] = val


def widen_call(plane, acts, meta):
    rows = acts[0].shape[0]
    return pl.pallas_call(
        widen,
        grid_spec=pltpu.PrefetchScalarGridSpec(
            num_scalar_prefetch=1,
            grid=(1,),
            in_specs=in_core(SIDE + 1),
            out_specs=in_core(6),
        ),
        out_shape=[pltpu.VMEM((SIDE * rows, COLS), BF)] * 6,
        compiler_params=params(8),
    )(plane, *map(near_core, (*acts, meta)))


def goals(z, x, core):
    spots = []
    for b in range(16):
        far, close = FAR[b // SIDE], b % SIDE
        by_z = jnp.where(core == 0, far, close)
        by_x = jnp.where(core == 0, close, far)
        spots.append(((z - by_z) & 3) * SIDE + ((x - by_x) & 3))
    return spots


def terms(plane_ref, z_ref, x_ref, core_ref, *refs):
    acts, meta_ref, route_ref, mats = refs[:SIDE], refs[SIDE], refs[SIDE + 1], refs[SIDE + 2:-5]
    sent_ref, wide_ref, out_ref, sort_ref, out_sems = refs[-5:]
    lead, rows = SIDE, acts[0].shape[0]
    deep = out_ref.shape[2] - LANES
    chunk = 256
    count = deep // chunk
    cuts = [slice(c * chunk, (c + 1) * chunk) for c in range(count)] + [slice(deep, deep + LANES)]
    stores = [
        pltpu.make_async_copy(out_ref.at[:, :, cut], sent_ref.at[:, :, cut], out_sems.at[c])
        for c, cut in enumerate(cuts)
    ]
    width = acts[0].shape[1]
    spots = goals(z_ref[0], x_ref[0], core_ref[0])
    for k in range(lead):
        home = (plane_ref[0] - k) & 3
        vals, meta = acts[k][...].astype(F32), meta_ref[home].astype(F32)
        route = route_ref[...].astype(F32) if k == 0 else jnp.zeros((rows, LANES), F32)
        for b in range(16):
            at = b * 8
            spot = pl.ds(pl.multiple_of(home * rows + spots[b] * 8, 8), 8)
            sort_ref[spot, :width] = vals[at:at + 8]
            sort_ref[spot, width:width + LANES] = meta[at:at + 8]
            sort_ref[spot, width + LANES:] = route[at:at + 8]
    moved = sort_ref[:, :width], sort_ref[:, width:width + LANES]
    for n, val in enumerate(dense(*moved, (0, 1, 3, 4))):
        wide_ref[:, n * COLS:(n + 1) * COLS] = val
    out_ref[:, :, cuts[-1]] = sort_ref[:, width + LANES:].astype(BF).reshape(lead, rows, LANES)
    stores[-1].start()
    for c in range(count):
        mat = jnp.concatenate([m[:, cuts[c]] for m in mats], axis=0)
        total = jnp.dot(wide_ref[...], mat, preferred_element_type=F32)
        out_ref[:, :, cuts[c]] = total.astype(BF).reshape(lead, rows, chunk)
        stores[c].start()
    for copy in stores:
        copy.wait()


def terms_call(spots, acts, meta, route, mats):
    lead, rows = SIDE, acts[0].shape[0]
    deep = mats[0].shape[1]
    out = (lead, rows, deep + LANES)
    chunk = 256
    outer = pl.BlockSpec(memory_space=pl.ANY)
    return pl.pallas_call(
        terms,
        grid_spec=pltpu.PrefetchScalarGridSpec(
            num_scalar_prefetch=4,
            grid=(1,),
            in_specs=in_core(SIDE + 6),
            out_specs=outer,
            scratch_shapes=[
                pltpu.VMEM((lead * rows, 4 * COLS), BF),
                pltpu.VMEM(out, BF),
                pltpu.VMEM((lead * rows, 8 * LANES), F32),
                pltpu.SemaphoreType.DMA((deep // chunk + 1,)),
            ],
        ),
        out_shape=pltpu.HBM(out, BF),
        compiler_params=params(16),
    )(*spots, *map(near_core, (*acts, meta, route, *mats)))


def finish(parts_ref, token_ref, route_ref):
    rows, width = parts_ref.shape[1:]
    deep = width - LANES
    group = parts_ref.shape[0] // SIDE
    route = jnp.zeros((rows, LANES), F32)
    for j in range(SIDE):
        total = jnp.zeros((rows, width), F32)
        for n in range(group):
            total = total + parts_ref[j * group + n].astype(F32)
        token_ref[:, j * deep:(j + 1) * deep] = total[:, :deep].astype(BF)
        route = route + total[:, deep:]
    eye = lax.broadcasted_iota(jnp.int32, (rows, rows), 0) == lax.broadcasted_iota(
        jnp.int32, (rows, rows), 1
    )
    for k in range(2):
        column = route[:, k:k + 1]
        route_ref[k:k + 1, :] = jnp.sum(jnp.where(eye, column, 0.0), axis=0, keepdims=True)


def finish_call(parts, deep):
    _, rows, _ = parts.shape
    return pl.pallas_call(
        finish,
        in_specs=in_core(1),
        out_shape=[
            jax.ShapeDtypeStruct((rows, deep * SIDE), BF),
            jax.ShapeDtypeStruct((2, rows), F32),
        ],
        compiler_params=params(8),
    )(near_core(parts))


def place(z, x, core):
    return (z % SIDE) * 8 + (x % SIDE) * 2 + core


def shift(arr, stage, by):
    pairs = []
    for z in range(SIDE):
        for x in range(SIDE):
            for core in range(2):
                along_x = core == stage
                goal = place(z, x + by, core) if along_x else place(z + by, x, core)
                pairs.append((place(z, x, core), goal))
    return lax.ppermute(arr, PLANE, pairs)


def turn(arr, by):
    return lax.ppermute(arr, "ep", [(i, (i + by) % SIDE) for i in range(SIDE)])


def swap(arr):
    return lax.ppermute(arr, "core", [(0, 1), (1, 0)])


def contract_rows(left, right):
    return lax.dot_general(left, right, (((0,), (0,)), ((), ())), preferred_element_type=F32)


def local(tokens, cotangent, routing, route_gates, gate_weight, up_weight, down_weight):
    tok_rows, _ = tokens.shape
    width = gate_weight.shape[2]
    own_mats = [w.reshape(COLS, width) for w in (gate_weight, up_weight, down_weight)]
    their_mats = [swap(w) for w in own_mats]
    mats = load_call(own_mats + their_mats)
    plane, *spot = (
        lax.axis_index(a).astype(jnp.int32).reshape(1) for a in ("ep",) + PLANE
    )
    send = pack_call((plane, *spot), tokens, cotangent, routing, route_gates, width)
    own = lax.all_to_all(send, "ep", 0, 0, tiled=True)
    near = [own] + [shift(own, 0, s) for s in range(1, SIDE)]
    lap = width + LANES
    x_0, y_0 = stack_call(near, lap)
    x_1 = shift(x_0, 1, 1)
    y_3 = shift(y_0, 1, 3)
    x_3 = shift(x_0, 1, 3)
    y_1 = shift(y_0, 1, 1)
    x_2 = shift(x_1, 1, 1)
    y_2 = shift(y_3, 1, 3)
    state = pre_call(plane, [x_0, y_0], mats, 2, SIDE, [])
    state = pre_call(plane, [x_1, x_3, y_1, y_3], mats, 0, SIDE, state)
    *parts, x_rows, y_rows, meta_rows = pre_call(plane, [x_2, y_2], mats, 3, SIDE, state)
    parts = [parts[0]] + [turn(parts[k], k) for k in range(1, SIDE)]
    done, route = middle_call(plane, parts, meta_rows)
    acts = [done] + [turn(done, k) for k in range(1, SIDE)]
    pair_mats = load_call(own_mats[:2] + their_mats[:2])
    sent = terms_call((plane, *spot), acts, meta_rows, route, pair_mats)
    got = lax.all_to_all(sent.reshape(-1, tok_rows, lap), TORUS, 0, 0, tiled=True)
    wides = widen_call(plane, acts, meta_rows)
    token_grad, route_sum = finish_call(got, width)
    route_grad = route_sum.T
    x_rows, y_rows = (r.reshape(-1, width) for r in (x_rows, y_rows))
    grads = []
    for m in range(3):
        rows = y_rows if m == 2 else x_rows
        theirs = swap(contract_rows(wides[3 + m], rows).astype(BF))
        mine = contract_rows(wides[m], rows) + theirs.astype(F32)
        grads.append(mine.astype(BF).reshape(gate_weight.shape))
    return (token_grad, route_grad, *grads)


def solution(mesh):
    names = ("ep", "z", "x", "core")
    fine = Mesh(mesh.devices.reshape(SIDE, SIDE, SIDE, 2), names)
    rows = P(names, None)
    mats = P(None, PLANE, "ep")

    return jax.shard_map(
        local,
        mesh=fine,
        in_specs=(rows, rows, rows, rows, mats, mats, mats),
        out_specs=(rows, rows, mats, mats, mats),
        check_vma=False,
    )
```

```python
import jax
import jax.numpy as jnp
from jax import lax
from jax.experimental import pallas as pl
from jax.experimental.pallas import tpu as pltpu
from jax.sharding import Mesh
from jax.sharding import PartitionSpec as P

BF = jnp.bfloat16
F32 = jnp.float32
EXPERTS = 8
HID = 64
COLS = EXPERTS * HID
LANES = 128
SIDE = 4
FAR = (1, 3, 0, 2)
PLANE = ("z", "x", "core")
TORUS = ("ep", "z", "x")


def params(mib):
    return pltpu.CompilerParams(vmem_limit_bytes=mib << 20)


def near_core(arr):
    return pltpu.with_memory_space_constraint(arr, pltpu.VMEM)


def far_off(arr):
    return pltpu.with_memory_space_constraint(arr, pltpu.HBM)


def in_core(count):
    return [pl.BlockSpec(memory_space=pltpu.VMEM)] * count


def first_half(rows):
    return lax.broadcasted_iota(jnp.int32, (rows, LANES), 1) < HID


def dot_t(rows, mat):
    return lax.dot_general(rows, mat, (((1,), (1,)), ((), ())), preferred_element_type=F32)


def dot_n(rows, mat):
    return jnp.dot(rows, mat, preferred_element_type=F32)


def flat(ref):
    lead, rows, width = ref.shape
    return ref[...].reshape(lead * rows, width)


def pack(plane_ref, z_ref, chip_ref, core_ref, tok_ref, cot_ref, route_ref, gates_ref, out_ref):
    rows, full = tok_ref.shape
    width = full // SIDE
    lap = width + LANES
    eye = lax.broadcasted_iota(jnp.int32, (rows, rows), 0) == lax.broadcasted_iota(
        jnp.int32, (rows, rows), 1
    )
    lane = lax.broadcasted_iota(jnp.int32, (rows, LANES), 1)
    meta = jnp.zeros((rows, LANES), F32)
    for n, ref in enumerate((route_ref, gates_ref)):
        vals = ref[...].astype(F32)
        for k in range(2):
            column = jnp.sum(jnp.where(eye, vals[k:k + 1, :], 0.0), axis=1, keepdims=True)
            meta = jnp.where(lane == 2 * n + k, column, meta)
    meta = meta.astype(BF)
    for j in range(SIDE):
        out_ref[j, :, :width] = tok_ref[:, j * width:(j + 1) * width]
        out_ref[j, :, width:lap] = meta
        out_ref[j, :, lap:] = cot_ref[:, j * width:(j + 1) * width]


def pack_call(spot, tokens, cotangent, routing, gates, width):
    args = (tokens, cotangent, routing.T, gates.T)
    rows = tokens.shape[0]
    out = pltpu.HBM((SIDE, rows, 2 * width + LANES), BF)
    return pl.pallas_call(
        pack,
        grid_spec=pltpu.PrefetchScalarGridSpec(
            num_scalar_prefetch=4,
            grid=(1,),
            in_specs=[pl.BlockSpec(a.shape, lambda i, *s: (0, 0)) for a in args],
            out_specs=pl.BlockSpec(out.shape, lambda i, *s: (0, 0, 0)),
        ),
        out_shape=out,
        compiler_params=params(8),
    )(*spot, *map(far_off, args))


def load(*refs):
    count = len(refs) // 2
    mats, outs, sems = refs[:count], refs[count:2 * count], refs[-1]
    copies = [pltpu.make_async_copy(mats[m], outs[m], sems.at[m]) for m in range(count)]
    for copy in copies:
        copy.start()
    for copy in copies:
        copy.wait()


def load_call(mats):
    return pl.pallas_call(
        load,
        in_specs=[pl.BlockSpec(memory_space=pl.ANY)] * len(mats),
        out_specs=in_core(len(mats)),
        out_shape=[pltpu.VMEM(m.shape, BF) for m in mats],
        scratch_shapes=[pltpu.SemaphoreType.DMA((len(mats),))],
        compiler_params=params(2),
    )(*map(far_off, mats))


def flip(*refs):
    count = len(refs) // 2
    for m in range(count):
        refs[count + m][...] = refs[m][...].T


def flip_call(mats):
    return pl.pallas_call(
        flip,
        in_specs=in_core(len(mats)),
        out_specs=in_core(len(mats)),
        out_shape=[pltpu.VMEM(m.shape[::-1], BF) for m in mats],
        compiler_params=params(8),
    )(*map(near_core, mats))


def stack(*refs):
    pieces, x_ref, y_ref = refs[:SIDE], refs[SIDE], refs[SIDE + 1]
    lap, rows = x_ref.shape[2], pieces[0].shape[1]
    for n, piece in enumerate(pieces):
        x_ref[:, n * rows:(n + 1) * rows, :] = piece[:, :, :lap]
        y_ref[:, n * rows:(n + 1) * rows, :] = piece[:, :, lap:]


def stack_call(pieces, lap):
    lead, rows, width = pieces[0].shape
    return pl.pallas_call(
        stack,
        in_specs=in_core(SIDE),
        out_specs=in_core(2),
        out_shape=[
            pltpu.VMEM((lead, SIDE * rows, lap), BF),
            pltpu.VMEM((lead, SIDE * rows, width - lap), BF),
        ],
        compiler_params=params(8),
    )(*map(near_core, pieces))


def pre_acts(count, first, width, multiply):
    def body(plane_ref, *refs):
        x_refs, y_refs, mats = refs[:count], refs[count:2 * count], refs[2 * count:2 * count + 6]
        *outs, x_out, y_out, meta_out, val_ref, sems, out_sems = refs[-10:]
        lead, short_rows = x_refs[0].shape[0], x_refs[0].shape[1]
        copies = []
        for n in range(count):
            rows_at = pl.ds(first + n * short_rows, short_rows)
            jobs = (
                (x_refs[n].at[:, :, :width], x_out.at[:, rows_at, :]),
                (y_refs[n], y_out.at[:, rows_at, :]),
                (x_refs[n].at[:, :, width:], meta_out.at[:, rows_at, :]),
            )
            for k, (src, dst) in enumerate(jobs):
                copies.append(pltpu.make_async_copy(src, dst, sems.at[n, k]))
        for copy in copies:
            copy.start()
        x_all = jnp.concatenate([flat(r) for r in x_refs], axis=0)
        y = jnp.concatenate([flat(r) for r in y_refs], axis=0)
        rows = y.shape[0]
        x, meta = x_all[:, :width], x_all[:, width:].astype(F32)
        lane = lax.broadcasted_iota(jnp.int32, (rows, COLS), 1)
        owner = (lane // HID).astype(F32)
        hit_a, hit_b = owner == meta[:, 0:1], owner == meta[:, 1:2]
        low = first_half(rows)
        for m in range(6):
            full = multiply(y if m % 3 == 2 else x, mats[m][...])
            sums = []
            for hit in (hit_a, hit_b):
                kept = jnp.where(hit, full, 0.0)
                short = sum(kept[:, g * LANES:(g + 1) * LANES] for g in range(COLS // LANES))
                sums.append(short + pltpu.roll(short, HID, 1))
            val = jnp.where(low, sums[0], sums[1]).astype(BF)
            for n in range(count):
                part = val[n * lead * short_rows:(n + 1) * lead * short_rows]
                part = part.reshape(lead, short_rows, LANES)
                val_ref[:, n * short_rows:(n + 1) * short_rows, m * LANES:(m + 1) * LANES] = part
        for k in range(lead):
            copy = pltpu.make_async_copy(
                val_ref.at[(plane_ref[0] + k) & 3],
                outs[k].at[pl.ds(first, count * short_rows), :],
                out_sems.at[k],
            )
            copy.start()
            copies.append(copy)
        for copy in copies:
            copy.wait()

    return body


def pre_call(plane, pieces, mats, multiply, first, total, into):
    count = len(pieces) // 2
    lead, rows, _ = pieces[0].shape
    width = pieces[-1].shape[2]
    outer = pl.BlockSpec(memory_space=pl.ANY)
    outs = [pltpu.HBM((rows * total, 6 * LANES), BF)] * lead
    outs = outs + [pltpu.HBM((lead, rows * total, w), BF) for w in (width, width, LANES)]
    taken = len(pieces) + 6
    return pl.pallas_call(
        pre_acts(count, first * rows, width, multiply),
        grid_spec=pltpu.PrefetchScalarGridSpec(
            num_scalar_prefetch=1,
            grid=(1,),
            in_specs=in_core(taken) + [outer] * len(into),
            out_specs=[outer] * len(outs),
            scratch_shapes=[
                pltpu.VMEM((lead, rows * count, 6 * LANES), BF),
                pltpu.SemaphoreType.DMA((count, 3)),
                pltpu.SemaphoreType.DMA((lead,)),
            ],
        ),
        out_shape=outs,
        input_output_aliases={1 + taken + n: n for n in range(len(into))},
        compiler_params=params(14),
    )(plane, *map(near_core, pieces), *map(near_core, mats), *map(far_off, into))


def middle(plane_ref, *refs):
    parts, meta_ref, out_ref, route_ref = refs[:SIDE], *refs[SIDE:]
    rows = out_ref.shape[0]
    meta = meta_ref[...].reshape(rows, LANES).astype(F32)
    low = first_half(rows)
    factor = jnp.where(low, meta[:, 2:3], meta[:, 3:4])
    prod = jnp.zeros((rows, LANES), F32)
    for side in range(2):
        vals = []
        for m in range(3):
            at = (3 * side + m) * LANES
            vals.append(sum(part[:, at:at + LANES].astype(F32) for part in parts))
        gate, upper, reverse = vals
        sigma = jax.nn.sigmoid(gate)
        act = gate * sigma
        hidden = (act * upper).astype(BF).astype(F32)
        back = factor * reverse
        d_gate = back * upper * sigma * (1.0 + gate * (1.0 - sigma))
        at = 3 * side * LANES
        for n, val in enumerate((d_gate, back * act, factor * hidden)):
            out_ref[:, at + n * LANES:at + (n + 1) * LANES] = val.astype(BF)
        prod = prod + hidden * reverse
    term_a = jnp.sum(jnp.where(low, prod, 0.0), axis=1, keepdims=True)
    term_b = jnp.sum(jnp.where(low, 0.0, prod), axis=1, keepdims=True)
    lane = lax.broadcasted_iota(jnp.int32, (rows, LANES), 1)
    route_ref[...] = jnp.where(lane == 0, term_a, jnp.where(lane == 1, term_b, 0.0)).astype(BF)


def middle_call(plane, parts, meta):
    rows, width = parts[0].shape
    return pl.pallas_call(
        middle,
        grid_spec=pltpu.PrefetchScalarGridSpec(
            num_scalar_prefetch=1,
            grid=(1,),
            in_specs=[pl.BlockSpec((rows, width), lambda i, s: (0, 0))]
            + in_core(SIDE - 1)
            + [pl.BlockSpec((1, rows, LANES), lambda i, s: (s[0], 0, 0))],
            out_specs=in_core(2),
        ),
        out_shape=[pltpu.VMEM((rows, width), BF), pltpu.VMEM((rows, LANES), BF)],
        compiler_params=params(6),
    )(plane, far_off(parts[0]), *map(near_core, parts[1:]), far_off(meta))


def spread(short, route_a, route_b, owner, low):
    turned = pltpu.roll(short, HID, 1)
    val_a = jnp.where(low, short, turned)
    val_b = jnp.where(low, turned, short)
    groups = COLS // LANES
    wide_a = jnp.concatenate([val_a] * groups, axis=1)
    wide_b = jnp.concatenate([val_b] * groups, axis=1)
    return jnp.where(owner == route_a, wide_a, jnp.where(owner == route_b, wide_b, 0.0))


def dense(acts, meta, picks):
    rows = meta.shape[0]
    lane = lax.broadcasted_iota(jnp.int32, (rows, COLS), 1)
    owner, low = (lane // HID).astype(F32), first_half(rows)
    return [
        spread(
            acts[:, m * LANES:(m + 1) * LANES], meta[:, 0:1], meta[:, 1:2], owner, low
        ).astype(BF)
        for m in picks
    ]


def widen(plane_ref, *refs):
    acts, meta_ref, outs = refs[:SIDE], refs[SIDE], refs[SIDE + 1:]
    rows = acts[0].shape[0]
    for k, ref in enumerate(acts):
        home = (plane_ref[0] - k) & 3
        vals = dense(ref[...].astype(F32), meta_ref[home].astype(F32), range(6))
        for out, val in zip(outs, vals):
            out[pl.ds(pl.multiple_of(home * rows, rows), rows), :] = val


def widen_call(plane, acts, meta):
    rows = acts[0].shape[0]
    return pl.pallas_call(
        widen,
        grid_spec=pltpu.PrefetchScalarGridSpec(
            num_scalar_prefetch=1,
            grid=(1,),
            in_specs=in_core(SIDE + 1),
            out_specs=in_core(6),
        ),
        out_shape=[pltpu.VMEM((SIDE * rows, COLS), BF)] * 6,
        compiler_params=params(8),
    )(plane, *map(near_core, (*acts, meta)))


def goals(z, x, core):
    spots = []
    for b in range(16):
        far, close = FAR[b // SIDE], b % SIDE
        by_z = jnp.where(core == 0, far, close)
        by_x = jnp.where(core == 0, close, far)
        spots.append(((z - by_z) & 3) * SIDE + ((x - by_x) & 3))
    return spots


def terms(plane_ref, z_ref, x_ref, core_ref, *refs):
    acts, meta_ref, route_ref, mats = refs[:SIDE], refs[SIDE], refs[SIDE + 1], refs[SIDE + 2:-5]
    sent_ref, wide_ref, out_ref, sort_ref, out_sems = refs[-5:]
    lead, rows = SIDE, acts[0].shape[0]
    deep = out_ref.shape[2] - LANES
    chunk = 256
    count = deep // chunk
    cuts = [slice(c * chunk, (c + 1) * chunk) for c in range(count)] + [slice(deep, deep + LANES)]
    stores = [
        pltpu.make_async_copy(out_ref.at[:, :, cut], sent_ref.at[:, :, cut], out_sems.at[c])
        for c, cut in enumerate(cuts)
    ]
    width = acts[0].shape[1]
    spots = goals(z_ref[0], x_ref[0], core_ref[0])
    for k in range(lead):
        home = (plane_ref[0] - k) & 3
        vals, meta = acts[k][...].astype(F32), meta_ref[home].astype(F32)
        route = route_ref[...].astype(F32) if k == 0 else jnp.zeros((rows, LANES), F32)
        for b in range(16):
            at = b * 8
            spot = pl.ds(pl.multiple_of(home * rows + spots[b] * 8, 8), 8)
            sort_ref[spot, :width] = vals[at:at + 8]
            sort_ref[spot, width:width + LANES] = meta[at:at + 8]
            sort_ref[spot, width + LANES:] = route[at:at + 8]
    moved = sort_ref[:, :width], sort_ref[:, width:width + LANES]
    for n, val in enumerate(dense(*moved, (0, 1, 3, 4))):
        wide_ref[:, n * COLS:(n + 1) * COLS] = val
    out_ref[:, :, cuts[-1]] = sort_ref[:, width + LANES:].astype(BF).reshape(lead, rows, LANES)
    stores[-1].start()
    for c in range(count):
        mat = jnp.concatenate([m[:, cuts[c]] for m in mats], axis=0)
        total = jnp.dot(wide_ref[...], mat, preferred_element_type=F32)
        out_ref[:, :, cuts[c]] = total.astype(BF).reshape(lead, rows, chunk)
        stores[c].start()
    for copy in stores:
        copy.wait()


def terms_call(spots, acts, meta, route, mats):
    lead, rows = SIDE, acts[0].shape[0]
    deep = mats[0].shape[1]
    out = (lead, rows, deep + LANES)
    chunk = 256
    outer = pl.BlockSpec(memory_space=pl.ANY)
    return pl.pallas_call(
        terms,
        grid_spec=pltpu.PrefetchScalarGridSpec(
            num_scalar_prefetch=4,
            grid=(1,),
            in_specs=in_core(SIDE + 6),
            out_specs=outer,
            scratch_shapes=[
                pltpu.VMEM((lead * rows, 4 * COLS), BF),
                pltpu.VMEM(out, BF),
                pltpu.VMEM((lead * rows, 8 * LANES), F32),
                pltpu.SemaphoreType.DMA((deep // chunk + 1,)),
            ],
        ),
        out_shape=pltpu.HBM(out, BF),
        compiler_params=params(16),
    )(*spots, *map(near_core, (*acts, meta, route, *mats)))


def finish(parts_ref, token_ref, route_ref):
    rows, width = parts_ref.shape[1:]
    deep = width - LANES
    group = parts_ref.shape[0] // SIDE
    route = jnp.zeros((rows, LANES), F32)
    for j in range(SIDE):
        total = jnp.zeros((rows, width), F32)
        for n in range(group):
            total = total + parts_ref[j * group + n].astype(F32)
        token_ref[:, j * deep:(j + 1) * deep] = total[:, :deep].astype(BF)
        route = route + total[:, deep:]
    eye = lax.broadcasted_iota(jnp.int32, (rows, rows), 0) == lax.broadcasted_iota(
        jnp.int32, (rows, rows), 1
    )
    for k in range(2):
        column = route[:, k:k + 1]
        route_ref[k:k + 1, :] = jnp.sum(jnp.where(eye, column, 0.0), axis=0, keepdims=True)


def finish_call(parts, deep):
    _, rows, _ = parts.shape
    return pl.pallas_call(
        finish,
        in_specs=in_core(1),
        out_shape=[
            jax.ShapeDtypeStruct((rows, deep * SIDE), BF),
            jax.ShapeDtypeStruct((2, rows), F32),
        ],
        compiler_params=params(8),
    )(near_core(parts))


def place(z, x, core):
    return (z % SIDE) * 8 + (x % SIDE) * 2 + core


def shift(arr, stage, by):
    pairs = []
    for z in range(SIDE):
        for x in range(SIDE):
            for core in range(2):
                along_x = core == stage
                goal = place(z, x + by, core) if along_x else place(z + by, x, core)
                pairs.append((place(z, x, core), goal))
    return lax.ppermute(arr, PLANE, pairs)


def turn(arr, by):
    return lax.ppermute(arr, "ep", [(i, (i + by) % SIDE) for i in range(SIDE)])


def swap(arr):
    return lax.ppermute(arr, "core", [(0, 1), (1, 0)])


def contract_rows(left, right):
    return lax.dot_general(left, right, (((0,), (0,)), ((), ())), preferred_element_type=F32)


def local(tokens, cotangent, routing, route_gates, gate_weight, up_weight, down_weight):
    tok_rows, _ = tokens.shape
    width = gate_weight.shape[2]
    own_mats = [w.reshape(COLS, width) for w in (gate_weight, up_weight, down_weight)]
    their_mats = [swap(w) for w in own_mats]
    mats = load_call(own_mats + their_mats)
    plane, *spot = (
        lax.axis_index(a).astype(jnp.int32).reshape(1) for a in ("ep",) + PLANE
    )
    send = pack_call((plane, *spot), tokens, cotangent, routing, route_gates, width)
    own = lax.all_to_all(send, "ep", 0, 0, tiled=True)
    near = [own] + [shift(own, 0, s) for s in range(1, SIDE)]
    lap = width + LANES
    x_0, y_0 = stack_call(near, lap)
    x_1 = shift(x_0, 1, 1)
    y_3 = shift(y_0, 1, 3)
    x_3 = shift(x_0, 1, 3)
    y_1 = shift(y_0, 1, 1)
    x_2 = shift(x_1, 1, 1)
    y_2 = shift(y_3, 1, 3)
    state = pre_call(plane, [x_0, y_0], mats, dot_t, 2, SIDE, [])
    flipped = flip_call(mats)
    state = pre_call(plane, [x_1, x_3, y_1, y_3], flipped, dot_n, 0, SIDE, state)
    *parts, x_rows, y_rows, meta_rows = pre_call(plane, [x_2, y_2], flipped, dot_n, 3, SIDE, state)
    parts = [parts[0]] + [turn(parts[k], k) for k in range(1, SIDE)]
    done, route = middle_call(plane, parts, meta_rows)
    acts = [done] + [turn(done, k) for k in range(1, SIDE)]
    pair_mats = load_call(own_mats[:2] + their_mats[:2])
    sent = terms_call((plane, *spot), acts, meta_rows, route, pair_mats)
    got = lax.all_to_all(sent.reshape(-1, tok_rows, lap), TORUS, 0, 0, tiled=True)
    wides = widen_call(plane, acts, meta_rows)
    token_grad, route_sum = finish_call(got, width)
    route_grad = route_sum.T
    x_rows, y_rows = (r.reshape(-1, width) for r in (x_rows, y_rows))
    grads = []
    for m in range(3):
        rows = y_rows if m == 2 else x_rows
        theirs = swap(contract_rows(wides[3 + m], rows).astype(BF))
        mine = contract_rows(wides[m], rows) + theirs.astype(F32)
        grads.append(mine.astype(BF).reshape(gate_weight.shape))
    return (token_grad, route_grad, *grads)


def solution(mesh):
    names = ("ep", "z", "x", "core")
    fine = Mesh(mesh.devices.reshape(SIDE, SIDE, SIDE, 2), names)
    rows = P(names, None)
    mats = P(None, PLANE, "ep")

    return jax.shard_map(
        local,
        mesh=fine,
        in_specs=(rows, rows, rows, rows, mats, mats, mats),
        out_specs=(rows, rows, mats, mats, mats),
        check_vma=False,
    )
```

```python
import jax
import jax.numpy as jnp
from jax import lax
from jax.experimental import pallas as pl
from jax.experimental.pallas import tpu as pltpu
from jax.sharding import Mesh
from jax.sharding import PartitionSpec as P

BF = jnp.bfloat16
F32 = jnp.float32
EXPERTS = 8
HID = 64
COLS = EXPERTS * HID
LANES = 128
SIDE = 4
FAR = (1, 3, 0, 2)
PLANE = ("z", "x", "core")
TORUS = ("ep", "x", "z")


def params(mib):
    return pltpu.CompilerParams(vmem_limit_bytes=mib << 20)


def near_core(arr):
    return pltpu.with_memory_space_constraint(arr, pltpu.VMEM)


def far_off(arr):
    return pltpu.with_memory_space_constraint(arr, pltpu.HBM)


def in_core(count):
    return [pl.BlockSpec(memory_space=pltpu.VMEM)] * count


def first_half(rows):
    return lax.broadcasted_iota(jnp.int32, (rows, LANES), 1) < HID


def dot_t(rows, mat):
    return lax.dot_general(rows, mat, (((1,), (1,)), ((), ())), preferred_element_type=F32)


def dot_n(rows, mat):
    return jnp.dot(rows, mat, preferred_element_type=F32)


def flat(ref):
    lead, rows, width = ref.shape
    return ref[...].reshape(lead * rows, width)


def pack(plane_ref, z_ref, chip_ref, core_ref, tok_ref, cot_ref, route_ref, gates_ref, out_ref):
    rows, full = tok_ref.shape
    width = full // SIDE
    lap = width + LANES
    eye = lax.broadcasted_iota(jnp.int32, (rows, rows), 0) == lax.broadcasted_iota(
        jnp.int32, (rows, rows), 1
    )
    lane = lax.broadcasted_iota(jnp.int32, (rows, LANES), 1)
    meta = jnp.zeros((rows, LANES), F32)
    for n, ref in enumerate((route_ref, gates_ref)):
        vals = ref[...].astype(F32)
        for k in range(2):
            column = jnp.sum(jnp.where(eye, vals[k:k + 1, :], 0.0), axis=1, keepdims=True)
            meta = jnp.where(lane == 2 * n + k, column, meta)
    meta = meta.astype(BF)
    for j in range(SIDE):
        out_ref[j, :, :width] = tok_ref[:, j * width:(j + 1) * width]
        out_ref[j, :, width:lap] = meta
        out_ref[j, :, lap:] = cot_ref[:, j * width:(j + 1) * width]


def pack_call(spot, tokens, cotangent, routing, gates, width):
    args = (tokens, cotangent, routing.T, gates.T)
    rows = tokens.shape[0]
    out = pltpu.HBM((SIDE, rows, 2 * width + LANES), BF)
    return pl.pallas_call(
        pack,
        grid_spec=pltpu.PrefetchScalarGridSpec(
            num_scalar_prefetch=4,
            grid=(1,),
            in_specs=[pl.BlockSpec(a.shape, lambda i, *s: (0, 0)) for a in args],
            out_specs=pl.BlockSpec(out.shape, lambda i, *s: (0, 0, 0)),
        ),
        out_shape=out,
        compiler_params=params(8),
    )(*spot, *map(far_off, args))


def load(*refs):
    count = len(refs) // 2
    mats, outs, sems = refs[:count], refs[count:2 * count], refs[-1]
    copies = [pltpu.make_async_copy(mats[m], outs[m], sems.at[m]) for m in range(count)]
    for copy in copies:
        copy.start()
    for copy in copies:
        copy.wait()


def load_call(mats):
    return pl.pallas_call(
        load,
        in_specs=[pl.BlockSpec(memory_space=pl.ANY)] * len(mats),
        out_specs=in_core(len(mats)),
        out_shape=[pltpu.VMEM(m.shape, BF) for m in mats],
        scratch_shapes=[pltpu.SemaphoreType.DMA((len(mats),))],
        compiler_params=params(2),
    )(*map(far_off, mats))


def flip(*refs):
    count = len(refs) // 2
    for m in range(count):
        refs[count + m][...] = refs[m][...].T


def flip_call(mats):
    return pl.pallas_call(
        flip,
        in_specs=in_core(len(mats)),
        out_specs=in_core(len(mats)),
        out_shape=[pltpu.VMEM(m.shape[::-1], BF) for m in mats],
        compiler_params=params(8),
    )(*map(near_core, mats))


def stack(*refs):
    pieces, x_ref, y_ref = refs[:SIDE], refs[SIDE], refs[SIDE + 1]
    lap, rows = x_ref.shape[2], pieces[0].shape[1]
    for n, piece in enumerate(pieces):
        x_ref[:, n * rows:(n + 1) * rows, :] = piece[:, :, :lap]
        y_ref[:, n * rows:(n + 1) * rows, :] = piece[:, :, lap:]


def stack_call(pieces, lap):
    lead, rows, width = pieces[0].shape
    return pl.pallas_call(
        stack,
        in_specs=in_core(SIDE),
        out_specs=in_core(2),
        out_shape=[
            pltpu.VMEM((lead, SIDE * rows, lap), BF),
            pltpu.VMEM((lead, SIDE * rows, width - lap), BF),
        ],
        compiler_params=params(8),
    )(*map(near_core, pieces))


def pre_acts(count, first, width, multiply):
    def body(plane_ref, *refs):
        x_refs, y_refs, mats = refs[:count], refs[count:2 * count], refs[2 * count:2 * count + 6]
        *outs, x_out, y_out, meta_out, val_ref, sems, out_sems = refs[-10:]
        lead, short_rows = x_refs[0].shape[0], x_refs[0].shape[1]
        copies = []
        for n in range(count):
            rows_at = pl.ds(first + n * short_rows, short_rows)
            jobs = (
                (x_refs[n].at[:, :, :width], x_out.at[:, rows_at, :]),
                (y_refs[n], y_out.at[:, rows_at, :]),
                (x_refs[n].at[:, :, width:], meta_out.at[:, rows_at, :]),
            )
            for k, (src, dst) in enumerate(jobs):
                copies.append(pltpu.make_async_copy(src, dst, sems.at[n, k]))
        for copy in copies:
            copy.start()
        x_all = jnp.concatenate([flat(r) for r in x_refs], axis=0)
        y = jnp.concatenate([flat(r) for r in y_refs], axis=0)
        rows = y.shape[0]
        x, meta = x_all[:, :width], x_all[:, width:].astype(F32)
        lane = lax.broadcasted_iota(jnp.int32, (rows, COLS), 1)
        owner = (lane // HID).astype(F32)
        hit_a, hit_b = owner == meta[:, 0:1], owner == meta[:, 1:2]
        low = first_half(rows)
        for m in range(6):
            full = multiply(y if m % 3 == 2 else x, mats[m][...])
            sums = []
            for hit in (hit_a, hit_b):
                kept = jnp.where(hit, full, 0.0)
                short = sum(kept[:, g * LANES:(g + 1) * LANES] for g in range(COLS // LANES))
                sums.append(short + pltpu.roll(short, HID, 1))
            val = jnp.where(low, sums[0], sums[1]).astype(BF)
            for n in range(count):
                part = val[n * lead * short_rows:(n + 1) * lead * short_rows]
                part = part.reshape(lead, short_rows, LANES)
                val_ref[:, n * short_rows:(n + 1) * short_rows, m * LANES:(m + 1) * LANES] = part
        for k in range(lead):
            copy = pltpu.make_async_copy(
                val_ref.at[(plane_ref[0] + k) & 3],
                outs[k].at[pl.ds(first, count * short_rows), :],
                out_sems.at[k],
            )
            copy.start()
            copies.append(copy)
        for copy in copies:
            copy.wait()

    return body


def pre_call(plane, pieces, mats, multiply, first, total, into):
    count = len(pieces) // 2
    lead, rows, _ = pieces[0].shape
    width = pieces[-1].shape[2]
    outer = pl.BlockSpec(memory_space=pl.ANY)
    outs = [pltpu.HBM((rows * total, 6 * LANES), BF)] * lead
    outs = outs + [pltpu.HBM((lead, rows * total, w), BF) for w in (width, width, LANES)]
    taken = len(pieces) + 6
    return pl.pallas_call(
        pre_acts(count, first * rows, width, multiply),
        grid_spec=pltpu.PrefetchScalarGridSpec(
            num_scalar_prefetch=1,
            grid=(1,),
            in_specs=in_core(taken) + [outer] * len(into),
            out_specs=[outer] * len(outs),
            scratch_shapes=[
                pltpu.VMEM((lead, rows * count, 6 * LANES), BF),
                pltpu.SemaphoreType.DMA((count, 3)),
                pltpu.SemaphoreType.DMA((lead,)),
            ],
        ),
        out_shape=outs,
        input_output_aliases={1 + taken + n: n for n in range(len(into))},
        compiler_params=params(14),
    )(plane, *map(near_core, pieces), *map(near_core, mats), *map(far_off, into))


def middle(plane_ref, *refs):
    parts, meta_ref, out_ref, scaled_ref, route_ref = refs[:SIDE], *refs[SIDE:]
    rows = out_ref.shape[0]
    meta = meta_ref[...].reshape(rows, LANES).astype(F32)
    low = first_half(rows)
    factor = jnp.where(low, meta[:, 2:3], meta[:, 3:4])
    prod = jnp.zeros((rows, LANES), F32)
    for side in range(2):
        vals = []
        for m in range(3):
            at = (3 * side + m) * LANES
            vals.append(sum(part[:, at:at + LANES].astype(F32) for part in parts))
        gate, upper, reverse = vals
        sigma = jax.nn.sigmoid(gate)
        act = gate * sigma
        hidden = (act * upper).astype(BF).astype(F32)
        back = factor * reverse
        d_gate = back * upper * sigma * (1.0 + gate * (1.0 - sigma))
        for n, val in enumerate((d_gate, back * act)):
            at = (2 * side + n) * LANES
            out_ref[:, at:at + LANES] = val.astype(BF)
        scaled_ref[:, side * LANES:(side + 1) * LANES] = (factor * hidden).astype(BF)
        prod = prod + hidden * reverse
    term_a = jnp.sum(jnp.where(low, prod, 0.0), axis=1, keepdims=True)
    term_b = jnp.sum(jnp.where(low, 0.0, prod), axis=1, keepdims=True)
    lane = lax.broadcasted_iota(jnp.int32, (rows, LANES), 1)
    route_ref[...] = jnp.where(lane == 0, term_a, jnp.where(lane == 1, term_b, 0.0)).astype(BF)


def middle_call(plane, parts, meta):
    rows, width = parts[0].shape
    return pl.pallas_call(
        middle,
        grid_spec=pltpu.PrefetchScalarGridSpec(
            num_scalar_prefetch=1,
            grid=(1,),
            in_specs=[pl.BlockSpec((rows, width), lambda i, s: (0, 0))]
            + in_core(SIDE - 1)
            + [pl.BlockSpec((1, rows, LANES), lambda i, s: (s[0], 0, 0))],
            out_specs=in_core(3),
        ),
        out_shape=[pltpu.VMEM((rows, w), BF) for w in (4 * LANES, 2 * LANES, LANES)],
        compiler_params=params(6),
    )(plane, far_off(parts[0]), *map(near_core, parts[1:]), far_off(meta))


def spread(short, route_a, route_b, owner, low):
    turned = pltpu.roll(short, HID, 1)
    val_a = jnp.where(low, short, turned)
    val_b = jnp.where(low, turned, short)
    groups = COLS // LANES
    wide_a = jnp.concatenate([val_a] * groups, axis=1)
    wide_b = jnp.concatenate([val_b] * groups, axis=1)
    return jnp.where(owner == route_a, wide_a, jnp.where(owner == route_b, wide_b, 0.0))


def dense(acts, meta, picks):
    rows = meta.shape[0]
    lane = lax.broadcasted_iota(jnp.int32, (rows, COLS), 1)
    owner, low = (lane // HID).astype(F32), first_half(rows)
    return [
        spread(
            acts[:, m * LANES:(m + 1) * LANES], meta[:, 0:1], meta[:, 1:2], owner, low
        ).astype(BF)
        for m in picks
    ]


def widen(plane_ref, *refs):
    acts, scales, meta_ref, outs = refs[:SIDE], refs[SIDE:-7], refs[-7], refs[-6:]
    rows = acts[0].shape[0]
    for k in range(SIDE):
        home = (plane_ref[0] - k) & 3
        meta = meta_ref[home].astype(F32)
        vals = dense(acts[k][...].astype(F32), meta, range(4))
        vals += dense(scales[k][...].astype(F32), meta, range(2))
        for out, val in zip(outs, vals):
            out[pl.ds(pl.multiple_of(home * rows, rows), rows), :] = val


def widen_call(plane, acts, scales, meta):
    rows = acts[0].shape[0]
    return pl.pallas_call(
        widen,
        grid_spec=pltpu.PrefetchScalarGridSpec(
            num_scalar_prefetch=1,
            grid=(1,),
            in_specs=in_core(2 * SIDE + 1),
            out_specs=in_core(6),
        ),
        out_shape=[pltpu.VMEM((SIDE * rows, COLS), BF)] * 6,
        compiler_params=params(8),
    )(plane, *map(near_core, (*acts, *scales, meta)))


def goals(z, x, core):
    spots = []
    for b in range(16):
        far, close = FAR[b // SIDE], b % SIDE
        by_z = jnp.where(core == 0, far, close)
        by_x = jnp.where(core == 0, close, far)
        spots.append(((x - by_x) & 3) * SIDE + ((z - by_z) & 3))
    return spots


def terms(plane_ref, z_ref, x_ref, core_ref, *refs):
    acts, meta_ref, route_ref, mats = refs[:SIDE], refs[SIDE], refs[SIDE + 1], refs[SIDE + 2:-5]
    sent_ref, wide_ref, out_ref, sort_ref, out_sems = refs[-5:]
    lead, rows = SIDE, acts[0].shape[0]
    deep = out_ref.shape[2] - LANES
    chunk = 256
    count = deep // chunk
    cuts = [slice(c * chunk, (c + 1) * chunk) for c in range(count)] + [slice(deep, deep + LANES)]
    stores = [
        pltpu.make_async_copy(out_ref.at[:, :, cut], sent_ref.at[:, :, cut], out_sems.at[c])
        for c, cut in enumerate(cuts)
    ]
    width = acts[0].shape[1]
    spots = goals(z_ref[0], x_ref[0], core_ref[0])
    for k in range(lead):
        home = (plane_ref[0] - k) & 3
        vals, meta = acts[k][...].astype(F32), meta_ref[home].astype(F32)
        route = route_ref[...].astype(F32) if k == 0 else jnp.zeros((rows, LANES), F32)
        for b in range(16):
            at = b * 8
            spot = pl.ds(pl.multiple_of(home * rows + spots[b] * 8, 8), 8)
            sort_ref[spot, :width] = vals[at:at + 8]
            sort_ref[spot, width:width + LANES] = meta[at:at + 8]
            sort_ref[spot, width + LANES:] = route[at:at + 8]
    moved = sort_ref[:, :width], sort_ref[:, width:width + LANES]
    for n, val in enumerate(dense(*moved, range(4))):
        wide_ref[:, n * COLS:(n + 1) * COLS] = val
    out_ref[:, :, cuts[-1]] = sort_ref[:, width + LANES:].astype(BF).reshape(lead, rows, LANES)
    stores[-1].start()
    for c in range(count):
        mat = jnp.concatenate([m[:, cuts[c]] for m in mats], axis=0)
        total = jnp.dot(wide_ref[...], mat, preferred_element_type=F32)
        out_ref[:, :, cuts[c]] = total.astype(BF).reshape(lead, rows, chunk)
        stores[c].start()
    for copy in stores:
        copy.wait()


def terms_call(spots, acts, meta, route, mats):
    lead, rows = SIDE, acts[0].shape[0]
    deep = mats[0].shape[1]
    out = (lead, rows, deep + LANES)
    chunk = 256
    outer = pl.BlockSpec(memory_space=pl.ANY)
    return pl.pallas_call(
        terms,
        grid_spec=pltpu.PrefetchScalarGridSpec(
            num_scalar_prefetch=4,
            grid=(1,),
            in_specs=in_core(SIDE + 6),
            out_specs=outer,
            scratch_shapes=[
                pltpu.VMEM((lead * rows, 4 * COLS), BF),
                pltpu.VMEM(out, BF),
                pltpu.VMEM((lead * rows, 6 * LANES), F32),
                pltpu.SemaphoreType.DMA((deep // chunk + 1,)),
            ],
        ),
        out_shape=pltpu.HBM(out, BF),
        compiler_params=params(16),
    )(*spots, *map(near_core, (*acts, meta, route, *mats)))


def finish(parts_ref, token_ref, route_ref):
    rows, width = parts_ref.shape[1:]
    deep = width - LANES
    group = parts_ref.shape[0] // SIDE
    route = jnp.zeros((rows, LANES), F32)
    for j in range(SIDE):
        total = jnp.zeros((rows, width), F32)
        for n in range(group):
            total = total + parts_ref[j * group + n].astype(F32)
        token_ref[:, j * deep:(j + 1) * deep] = total[:, :deep].astype(BF)
        route = route + total[:, deep:]
    eye = lax.broadcasted_iota(jnp.int32, (rows, rows), 0) == lax.broadcasted_iota(
        jnp.int32, (rows, rows), 1
    )
    for k in range(2):
        column = route[:, k:k + 1]
        route_ref[k:k + 1, :] = jnp.sum(jnp.where(eye, column, 0.0), axis=0, keepdims=True)


def finish_call(parts, deep):
    _, rows, _ = parts.shape
    return pl.pallas_call(
        finish,
        in_specs=in_core(1),
        out_shape=[
            jax.ShapeDtypeStruct((rows, deep * SIDE), BF),
            jax.ShapeDtypeStruct((2, rows), F32),
        ],
        compiler_params=params(8),
    )(near_core(parts))


def place(z, x, core):
    return (z % SIDE) * 8 + (x % SIDE) * 2 + core


def shift(arr, stage, by):
    pairs = []
    for z in range(SIDE):
        for x in range(SIDE):
            for core in range(2):
                along_x = core == stage
                goal = place(z, x + by, core) if along_x else place(z + by, x, core)
                pairs.append((place(z, x, core), goal))
    return lax.ppermute(arr, PLANE, pairs)


def turn(arr, by):
    return lax.ppermute(arr, "ep", [(i, (i + by) % SIDE) for i in range(SIDE)])


def swap(arr):
    return lax.ppermute(arr, "core", [(0, 1), (1, 0)])


def contract_rows(left, right):
    return lax.dot_general(left, right, (((0,), (0,)), ((), ())), preferred_element_type=F32)


def local(tokens, cotangent, routing, route_gates, gate_weight, up_weight, down_weight):
    tok_rows, _ = tokens.shape
    width = gate_weight.shape[2]
    own_mats = [w.reshape(COLS, width) for w in (gate_weight, up_weight, down_weight)]
    their_mats = [swap(w) for w in own_mats]
    mats = load_call(own_mats + their_mats)
    plane, *spot = (
        lax.axis_index(a).astype(jnp.int32).reshape(1) for a in ("ep",) + PLANE
    )
    send = pack_call((plane, *spot), tokens, cotangent, routing, route_gates, width)
    own = lax.all_to_all(send, "ep", 0, 0, tiled=True)
    near = [own] + [shift(own, 0, s) for s in range(1, SIDE)]
    lap = width + LANES
    x_0, y_0 = stack_call(near, lap)
    x_1 = shift(x_0, 1, 1)
    y_3 = shift(y_0, 1, 3)
    x_3 = shift(x_0, 1, 3)
    y_1 = shift(y_0, 1, 1)
    x_2 = shift(x_1, 1, 1)
    y_2 = shift(y_3, 1, 3)
    state = pre_call(plane, [x_0, y_0], mats, dot_t, 2, SIDE, [])
    flipped = flip_call(mats)
    state = pre_call(plane, [x_1, x_3, y_1, y_3], flipped, dot_n, 0, SIDE, state)
    *parts, x_rows, y_rows, meta_rows = pre_call(plane, [x_2, y_2], flipped, dot_n, 3, SIDE, state)
    parts = [parts[0]] + [turn(parts[k], k) for k in range(1, SIDE)]
    done, scaled, route = middle_call(plane, parts, meta_rows)
    acts = [done] + [turn(done, k) for k in range(1, SIDE)]
    scales = [scaled] + [turn(scaled, k) for k in range(1, SIDE)]
    pair_mats = load_call(own_mats[:2] + their_mats[:2])
    sent = terms_call((plane, *spot), acts, meta_rows, route, pair_mats)
    got = lax.all_to_all(sent.reshape(-1, tok_rows, lap), TORUS, 0, 0, tiled=True)
    wides = widen_call(plane, acts, scales, meta_rows)
    token_grad, route_sum = finish_call(got, width)
    route_grad = route_sum.T
    x_rows, y_rows = (r.reshape(-1, width) for r in (x_rows, y_rows))
    grads = []
    for m in range(3):
        rows = y_rows if m == 2 else x_rows
        theirs = swap(contract_rows(wides[(2, 3, 5)[m]], rows).astype(BF))
        mine = contract_rows(wides[(0, 1, 4)[m]], rows) + theirs.astype(F32)
        grads.append(mine.astype(BF).reshape(gate_weight.shape))
    return (token_grad, route_grad, *grads)


def solution(mesh):
    names = ("ep", "z", "x", "core")
    fine = Mesh(mesh.devices.reshape(SIDE, SIDE, SIDE, 2), names)
    rows = P(names, None)
    mats = P(None, PLANE, "ep")

    return jax.shard_map(
        local,
        mesh=fine,
        in_specs=(rows, rows, rows, rows, mats, mats, mats),
        out_specs=(rows, rows, mats, mats, mats),
        check_vma=False,
    )
```

```python
import jax
import jax.numpy as jnp
from jax import lax
from jax.experimental import pallas as pl
from jax.experimental.pallas import tpu as pltpu
from jax.sharding import Mesh
from jax.sharding import PartitionSpec as P

BF = jnp.bfloat16
F32 = jnp.float32
EXPERTS = 8
HID = 64
COLS = EXPERTS * HID
LANES = 128
SIDE = 4
FAR = (1, 3, 0, 2)
PLANE = ("z", "x", "core")
TORUS = ("ep", "x", "z")


def params(mib):
    return pltpu.CompilerParams(vmem_limit_bytes=mib << 20)


def near_core(arr):
    return pltpu.with_memory_space_constraint(arr, pltpu.VMEM)


def far_off(arr):
    return pltpu.with_memory_space_constraint(arr, pltpu.HBM)


def in_core(count):
    return [pl.BlockSpec(memory_space=pltpu.VMEM)] * count


def first_half(rows):
    return lax.broadcasted_iota(jnp.int32, (rows, LANES), 1) < HID


def dot_t(rows, mat):
    return lax.dot_general(rows, mat, (((1,), (1,)), ((), ())), preferred_element_type=F32)


def dot_n(rows, mat):
    return jnp.dot(rows, mat, preferred_element_type=F32)


def flat(ref):
    lead, rows, width = ref.shape
    return ref[...].reshape(lead * rows, width)


def pack(plane_ref, z_ref, chip_ref, core_ref, tok_ref, cot_ref, route_ref, gates_ref, *rest):
    out_ref, meta_ref, sems = rest
    rows, full = tok_ref.shape
    width = full // SIDE
    lap = width + LANES
    copies = []
    for j in range(SIDE):
        cut = slice(j * width, (j + 1) * width)
        jobs = (
            (tok_ref.at[:, cut], out_ref.at[j, :, :width]),
            (cot_ref.at[:, cut], out_ref.at[j, :, lap:]),
            (meta_ref, out_ref.at[j, :, width:lap]),
        )
        copies.append(
            [pltpu.make_async_copy(src, dst, sems.at[j, n]) for n, (src, dst) in enumerate(jobs)]
        )
    for group in copies:
        group[0].start()
        group[1].start()
    eye = lax.broadcasted_iota(jnp.int32, (rows, rows), 0) == lax.broadcasted_iota(
        jnp.int32, (rows, rows), 1
    )
    lane = lax.broadcasted_iota(jnp.int32, (rows, LANES), 1)
    meta = jnp.zeros((rows, LANES), F32)
    for n, ref in enumerate((route_ref, gates_ref)):
        vals = ref[...].astype(F32)
        for k in range(2):
            column = jnp.sum(jnp.where(eye, vals[k:k + 1, :], 0.0), axis=1, keepdims=True)
            meta = jnp.where(lane == 2 * n + k, column, meta)
    meta_ref[...] = meta.astype(BF)
    for group in copies:
        group[2].start()
    for group in copies:
        for copy in group:
            copy.wait()


def pack_call(spot, tokens, cotangent, routing, gates, width):
    args = (tokens, cotangent, routing.T, gates.T)
    rows = tokens.shape[0]
    out = pltpu.HBM((SIDE, rows, 2 * width + LANES), BF)
    return pl.pallas_call(
        pack,
        grid_spec=pltpu.PrefetchScalarGridSpec(
            num_scalar_prefetch=4,
            grid=(1,),
            in_specs=[pl.BlockSpec(memory_space=pl.ANY)] * 2
            + [pl.BlockSpec(a.shape, lambda i, *s: (0, 0)) for a in args[2:]],
            out_specs=pl.BlockSpec(memory_space=pl.ANY),
            scratch_shapes=[pltpu.VMEM((rows, LANES), BF), pltpu.SemaphoreType.DMA((SIDE, 3))],
        ),
        out_shape=out,
        compiler_params=params(8),
    )(*spot, *map(far_off, args))


def load(*refs):
    count = len(refs) // 2
    mats, outs, sems = refs[:count], refs[count:2 * count], refs[-1]
    copies = [pltpu.make_async_copy(mats[m], outs[m], sems.at[m]) for m in range(count)]
    for copy in copies:
        copy.start()
    for copy in copies:
        copy.wait()


def load_call(mats):
    return pl.pallas_call(
        load,
        in_specs=[pl.BlockSpec(memory_space=pl.ANY)] * len(mats),
        out_specs=in_core(len(mats)),
        out_shape=[pltpu.VMEM(m.shape, BF) for m in mats],
        scratch_shapes=[pltpu.SemaphoreType.DMA((len(mats),))],
        compiler_params=params(2),
    )(*map(far_off, mats))


def flip(*refs):
    count = len(refs) // 2
    for m in range(count):
        refs[count + m][...] = refs[m][...].T


def flip_call(mats):
    return pl.pallas_call(
        flip,
        in_specs=in_core(len(mats)),
        out_specs=in_core(len(mats)),
        out_shape=[pltpu.VMEM(m.shape[::-1], BF) for m in mats],
        compiler_params=params(8),
    )(*map(near_core, mats))


def stack(*refs):
    pieces, x_ref, y_ref = refs[:SIDE], refs[SIDE], refs[SIDE + 1]
    lap, rows = x_ref.shape[2], pieces[0].shape[1]
    for n, piece in enumerate(pieces):
        x_ref[:, n * rows:(n + 1) * rows, :] = piece[:, :, :lap]
        y_ref[:, n * rows:(n + 1) * rows, :] = piece[:, :, lap:]


def stack_call(pieces, lap):
    lead, rows, width = pieces[0].shape
    return pl.pallas_call(
        stack,
        in_specs=in_core(SIDE),
        out_specs=in_core(2),
        out_shape=[
            pltpu.VMEM((lead, SIDE * rows, lap), BF),
            pltpu.VMEM((lead, SIDE * rows, width - lap), BF),
        ],
        compiler_params=params(8),
    )(*map(near_core, pieces))


def pre_acts(count, first, width, multiply):
    def body(plane_ref, *refs):
        x_refs, y_refs, mats = refs[:count], refs[count:2 * count], refs[2 * count:2 * count + 6]
        *outs, x_out, y_out, meta_out, val_ref, sems, out_sems = refs[-10:]
        lead, short_rows = x_refs[0].shape[0], x_refs[0].shape[1]
        copies = []
        for n in range(count):
            rows_at = pl.ds(first + n * short_rows, short_rows)
            jobs = (
                (x_refs[n].at[:, :, :width], x_out.at[:, rows_at, :]),
                (y_refs[n], y_out.at[:, rows_at, :]),
                (x_refs[n].at[:, :, width:], meta_out.at[:, rows_at, :]),
            )
            for k, (src, dst) in enumerate(jobs):
                copies.append(pltpu.make_async_copy(src, dst, sems.at[n, k]))
        for copy in copies:
            copy.start()
        x_all = jnp.concatenate([flat(r) for r in x_refs], axis=0)
        y = jnp.concatenate([flat(r) for r in y_refs], axis=0)
        rows = y.shape[0]
        x, meta = x_all[:, :width], x_all[:, width:].astype(F32)
        lane = lax.broadcasted_iota(jnp.int32, (rows, COLS), 1)
        owner = (lane // HID).astype(F32)
        hit_a, hit_b = owner == meta[:, 0:1], owner == meta[:, 1:2]
        low = first_half(rows)
        for m in range(6):
            full = multiply(y if m % 3 == 2 else x, mats[m][...])
            sums = []
            for hit in (hit_a, hit_b):
                kept = jnp.where(hit, full, 0.0)
                short = sum(kept[:, g * LANES:(g + 1) * LANES] for g in range(COLS // LANES))
                sums.append(short + pltpu.roll(short, HID, 1))
            val = jnp.where(low, sums[0], sums[1]).astype(BF)
            for n in range(count):
                part = val[n * lead * short_rows:(n + 1) * lead * short_rows]
                part = part.reshape(lead, short_rows, LANES)
                val_ref[:, n * short_rows:(n + 1) * short_rows, m * LANES:(m + 1) * LANES] = part
        for k in range(lead):
            copy = pltpu.make_async_copy(
                val_ref.at[(plane_ref[0] + k) & 3],
                outs[k].at[pl.ds(first, count * short_rows), :],
                out_sems.at[k],
            )
            copy.start()
            copies.append(copy)
        for copy in copies:
            copy.wait()

    return body


def pre_call(plane, pieces, mats, multiply, first, total, into):
    count = len(pieces) // 2
    lead, rows, _ = pieces[0].shape
    width = pieces[-1].shape[2]
    outer = pl.BlockSpec(memory_space=pl.ANY)
    outs = [pltpu.HBM((rows * total, 6 * LANES), BF)] * lead
    outs = outs + [pltpu.HBM((lead, rows * total, w), BF) for w in (width, width, LANES)]
    taken = len(pieces) + 6
    return pl.pallas_call(
        pre_acts(count, first * rows, width, multiply),
        grid_spec=pltpu.PrefetchScalarGridSpec(
            num_scalar_prefetch=1,
            grid=(1,),
            in_specs=in_core(taken) + [outer] * len(into),
            out_specs=[outer] * len(outs),
            scratch_shapes=[
                pltpu.VMEM((lead, rows * count, 6 * LANES), BF),
                pltpu.SemaphoreType.DMA((count, 3)),
                pltpu.SemaphoreType.DMA((lead,)),
            ],
        ),
        out_shape=outs,
        input_output_aliases={1 + taken + n: n for n in range(len(into))},
        compiler_params=params(14),
    )(plane, *map(near_core, pieces), *map(near_core, mats), *map(far_off, into))


def middle(plane_ref, *refs):
    parts, meta_ref, out_ref, scaled_ref, route_ref = refs[:SIDE], *refs[SIDE:]
    rows = out_ref.shape[0]
    meta = meta_ref[...].reshape(rows, LANES).astype(F32)
    low = first_half(rows)
    factor = jnp.where(low, meta[:, 2:3], meta[:, 3:4])
    prod = jnp.zeros((rows, LANES), F32)
    for side in range(2):
        vals = []
        for m in range(3):
            at = (3 * side + m) * LANES
            vals.append(sum(part[:, at:at + LANES].astype(F32) for part in parts))
        gate, upper, reverse = vals
        sigma = jax.nn.sigmoid(gate)
        act = gate * sigma
        hidden = (act * upper).astype(BF).astype(F32)
        back = factor * reverse
        d_gate = back * upper * sigma * (1.0 + gate * (1.0 - sigma))
        for n, val in enumerate((d_gate, back * act)):
            at = (2 * side + n) * LANES
            out_ref[:, at:at + LANES] = val.astype(BF)
        scaled_ref[:, side * LANES:(side + 1) * LANES] = (factor * hidden).astype(BF)
        prod = prod + hidden * reverse
    term_a = jnp.sum(jnp.where(low, prod, 0.0), axis=1, keepdims=True)
    term_b = jnp.sum(jnp.where(low, 0.0, prod), axis=1, keepdims=True)
    lane = lax.broadcasted_iota(jnp.int32, (rows, LANES), 1)
    route_ref[...] = jnp.where(lane == 0, term_a, jnp.where(lane == 1, term_b, 0.0)).astype(BF)


def middle_call(plane, parts, meta):
    rows, width = parts[0].shape
    return pl.pallas_call(
        middle,
        grid_spec=pltpu.PrefetchScalarGridSpec(
            num_scalar_prefetch=1,
            grid=(1,),
            in_specs=[pl.BlockSpec((rows, width), lambda i, s: (0, 0))]
            + in_core(SIDE - 1)
            + [pl.BlockSpec((1, rows, LANES), lambda i, s: (s[0], 0, 0))],
            out_specs=in_core(3),
        ),
        out_shape=[pltpu.VMEM((rows, w), BF) for w in (4 * LANES, 2 * LANES, LANES)],
        compiler_params=params(6),
    )(plane, far_off(parts[0]), *map(near_core, parts[1:]), far_off(meta))


def spread(short, route_a, route_b, owner, low):
    turned = pltpu.roll(short, HID, 1)
    val_a = jnp.where(low, short, turned)
    val_b = jnp.where(low, turned, short)
    groups = COLS // LANES
    wide_a = jnp.concatenate([val_a] * groups, axis=1)
    wide_b = jnp.concatenate([val_b] * groups, axis=1)
    return jnp.where(owner == route_a, wide_a, jnp.where(owner == route_b, wide_b, 0.0))


def dense(acts, meta, picks):
    rows = meta.shape[0]
    lane = lax.broadcasted_iota(jnp.int32, (rows, COLS), 1)
    owner, low = (lane // HID).astype(F32), first_half(rows)
    return [
        spread(
            acts[:, m * LANES:(m + 1) * LANES], meta[:, 0:1], meta[:, 1:2], owner, low
        ).astype(BF)
        for m in picks
    ]


def widen(plane_ref, *refs):
    acts, scales, meta_ref, outs = refs[:SIDE], refs[SIDE:-7], refs[-7], refs[-6:]
    rows = acts[0].shape[0]
    for k in range(SIDE):
        home = (plane_ref[0] - k) & 3
        meta = meta_ref[home].astype(F32)
        vals = dense(acts[k][...].astype(F32), meta, range(4))
        vals += dense(scales[k][...].astype(F32), meta, range(2))
        for out, val in zip(outs, vals):
            out[pl.ds(pl.multiple_of(home * rows, rows), rows), :] = val


def widen_call(plane, acts, scales, meta):
    rows = acts[0].shape[0]
    return pl.pallas_call(
        widen,
        grid_spec=pltpu.PrefetchScalarGridSpec(
            num_scalar_prefetch=1,
            grid=(1,),
            in_specs=in_core(2 * SIDE + 1),
            out_specs=in_core(6),
        ),
        out_shape=[pltpu.VMEM((SIDE * rows, COLS), BF)] * 6,
        compiler_params=params(8),
    )(plane, *map(near_core, (*acts, *scales, meta)))


def goals(z, x, core):
    spots = []
    for b in range(16):
        far, close = FAR[b // SIDE], b % SIDE
        by_z = jnp.where(core == 0, far, close)
        by_x = jnp.where(core == 0, close, far)
        spots.append(((x - by_x) & 3) * SIDE + ((z - by_z) & 3))
    return spots


def terms(plane_ref, z_ref, x_ref, core_ref, *refs):
    acts, meta_ref, route_ref, mats = refs[:SIDE], refs[SIDE], refs[SIDE + 1], refs[SIDE + 2:-5]
    sent_ref, wide_ref, out_ref, sort_ref, out_sems = refs[-5:]
    lead, rows = SIDE, acts[0].shape[0]
    deep = out_ref.shape[2] - LANES
    chunk = 256
    count = deep // chunk
    cuts = [slice(c * chunk, (c + 1) * chunk) for c in range(count)] + [slice(deep, deep + LANES)]
    stores = [
        pltpu.make_async_copy(out_ref.at[:, :, cut], sent_ref.at[:, :, cut], out_sems.at[c])
        for c, cut in enumerate(cuts)
    ]
    width = acts[0].shape[1]
    spots = goals(z_ref[0], x_ref[0], core_ref[0])
    for k in range(lead):
        home = (plane_ref[0] - k) & 3
        vals, meta = acts[k][...].astype(F32), meta_ref[home].astype(F32)
        route = route_ref[...].astype(F32) if k == 0 else jnp.zeros((rows, LANES), F32)
        for b in range(16):
            at = b * 8
            spot = pl.ds(pl.multiple_of(home * rows + spots[b] * 8, 8), 8)
            sort_ref[spot, :width] = vals[at:at + 8]
            sort_ref[spot, width:width + LANES] = meta[at:at + 8]
            sort_ref[spot, width + LANES:] = route[at:at + 8]
    moved = sort_ref[:, :width], sort_ref[:, width:width + LANES]
    for n, val in enumerate(dense(*moved, range(4))):
        wide_ref[:, n * COLS:(n + 1) * COLS] = val
    out_ref[:, :, cuts[-1]] = sort_ref[:, width + LANES:].astype(BF).reshape(lead, rows, LANES)
    stores[-1].start()
    for c in range(count):
        mat = jnp.concatenate([m[:, cuts[c]] for m in mats], axis=0)
        total = jnp.dot(wide_ref[...], mat, preferred_element_type=F32)
        out_ref[:, :, cuts[c]] = total.astype(BF).reshape(lead, rows, chunk)
        stores[c].start()
    for copy in stores:
        copy.wait()


def terms_call(spots, acts, meta, route, mats):
    lead, rows = SIDE, acts[0].shape[0]
    deep = mats[0].shape[1]
    out = (lead, rows, deep + LANES)
    chunk = 256
    outer = pl.BlockSpec(memory_space=pl.ANY)
    return pl.pallas_call(
        terms,
        grid_spec=pltpu.PrefetchScalarGridSpec(
            num_scalar_prefetch=4,
            grid=(1,),
            in_specs=in_core(SIDE + 6),
            out_specs=outer,
            scratch_shapes=[
                pltpu.VMEM((lead * rows, 4 * COLS), BF),
                pltpu.VMEM(out, BF),
                pltpu.VMEM((lead * rows, 6 * LANES), F32),
                pltpu.SemaphoreType.DMA((deep // chunk + 1,)),
            ],
        ),
        out_shape=pltpu.HBM(out, BF),
        compiler_params=params(16),
    )(*spots, *map(near_core, (*acts, meta, route, *mats)))


def finish(parts_ref, token_ref, route_ref):
    rows, width = parts_ref.shape[1:]
    deep = width - LANES
    group = parts_ref.shape[0] // SIDE
    route = jnp.zeros((rows, LANES), F32)
    for j in range(SIDE):
        total = jnp.zeros((rows, width), F32)
        for n in range(group):
            total = total + parts_ref[j * group + n].astype(F32)
        token_ref[:, j * deep:(j + 1) * deep] = total[:, :deep].astype(BF)
        route = route + total[:, deep:]
    eye = lax.broadcasted_iota(jnp.int32, (rows, rows), 0) == lax.broadcasted_iota(
        jnp.int32, (rows, rows), 1
    )
    for k in range(2):
        column = route[:, k:k + 1]
        route_ref[k:k + 1, :] = jnp.sum(jnp.where(eye, column, 0.0), axis=0, keepdims=True)


def finish_call(parts, deep):
    _, rows, _ = parts.shape
    return pl.pallas_call(
        finish,
        in_specs=in_core(1),
        out_shape=[
            jax.ShapeDtypeStruct((rows, deep * SIDE), BF),
            jax.ShapeDtypeStruct((2, rows), F32),
        ],
        compiler_params=params(8),
    )(near_core(parts))


def place(z, x, core):
    return (z % SIDE) * 8 + (x % SIDE) * 2 + core


def shift(arr, stage, by):
    pairs = []
    for z in range(SIDE):
        for x in range(SIDE):
            for core in range(2):
                along_x = core == stage
                goal = place(z, x + by, core) if along_x else place(z + by, x, core)
                pairs.append((place(z, x, core), goal))
    return lax.ppermute(arr, PLANE, pairs)


def turn(arr, by):
    return lax.ppermute(arr, "ep", [(i, (i + by) % SIDE) for i in range(SIDE)])


def swap(arr):
    return lax.ppermute(arr, "core", [(0, 1), (1, 0)])


def contract_rows(left, right):
    return lax.dot_general(left, right, (((0,), (0,)), ((), ())), preferred_element_type=F32)


def local(tokens, cotangent, routing, route_gates, gate_weight, up_weight, down_weight):
    tok_rows, _ = tokens.shape
    width = gate_weight.shape[2]
    own_mats = [w.reshape(COLS, width) for w in (gate_weight, up_weight, down_weight)]
    their_mats = [swap(w) for w in own_mats]
    mats = load_call(own_mats + their_mats)
    plane, *spot = (
        lax.axis_index(a).astype(jnp.int32).reshape(1) for a in ("ep",) + PLANE
    )
    send = pack_call((plane, *spot), tokens, cotangent, routing, route_gates, width)
    own = lax.all_to_all(send, "ep", 0, 0, tiled=True)
    near = [own] + [shift(own, 0, s) for s in range(1, SIDE)]
    lap = width + LANES
    x_0, y_0 = stack_call(near, lap)
    x_1 = shift(x_0, 1, 1)
    y_3 = shift(y_0, 1, 3)
    x_3 = shift(x_0, 1, 3)
    y_1 = shift(y_0, 1, 1)
    x_2 = shift(x_1, 1, 1)
    y_2 = shift(y_3, 1, 3)
    state = pre_call(plane, [x_0, y_0], mats, dot_t, 2, SIDE, [])
    flipped = flip_call(mats)
    state = pre_call(plane, [x_1, x_3, y_1, y_3], flipped, dot_n, 0, SIDE, state)
    *parts, x_rows, y_rows, meta_rows = pre_call(plane, [x_2, y_2], flipped, dot_n, 3, SIDE, state)
    parts = [parts[0]] + [turn(parts[k], k) for k in range(1, SIDE)]
    done, scaled, route = middle_call(plane, parts, meta_rows)
    acts = [done] + [turn(done, k) for k in range(1, SIDE)]
    scales = [scaled] + [turn(scaled, k) for k in range(1, SIDE)]
    pair_mats = load_call(own_mats[:2] + their_mats[:2])
    sent = terms_call((plane, *spot), acts, meta_rows, route, pair_mats)
    got = lax.all_to_all(sent.reshape(-1, tok_rows, lap), TORUS, 0, 0, tiled=True)
    wides = widen_call(plane, acts, scales, meta_rows)
    token_grad, route_sum = finish_call(got, width)
    route_grad = route_sum.T
    x_rows, y_rows = (r.reshape(-1, width) for r in (x_rows, y_rows))
    grads = []
    for m in range(3):
        rows = y_rows if m == 2 else x_rows
        theirs = swap(contract_rows(wides[(2, 3, 5)[m]], rows).astype(BF))
        mine = contract_rows(wides[(0, 1, 4)[m]], rows) + theirs.astype(F32)
        grads.append(mine.astype(BF).reshape(gate_weight.shape))
    return (token_grad, route_grad, *grads)


def solution(mesh):
    names = ("ep", "z", "x", "core")
    fine = Mesh(mesh.devices.reshape(SIDE, SIDE, SIDE, 2), names)
    rows = P(names, None)
    mats = P(None, PLANE, "ep")

    return jax.shard_map(
        local,
        mesh=fine,
        in_specs=(rows, rows, rows, rows, mats, mats, mats),
        out_specs=(rows, rows, mats, mats, mats),
        check_vma=False,
    )
```
